256 devices in a mesh: owner: 64 (over z, x, core), col: 4 (over y).
Axes of the slice: x: 4, y: 4, z: 8, core: 2. Of those that a mesh axis runs over, the one named last changes fastest.
Arguments:
- momentum: float32 [128, 512, 2048], P(None, 'owner', 'col'), may hold values from -7200 to 7200
- hidden_acts: bfloat16 [32768, 512], P('owner'), may hold values from -6 to 6
- output_grads: bfloat16 [32768, 2048], P('owner', 'col'), may hold values from -6 to 6
- routing: int32 [32768], P('owner'), may hold values from 0 to 1
- assignment: int32 [128], replicated, may hold values from 0 to 127, each once
Outputs:
- new_momentum: float32 [128, 512, 2048], P(None, 'owner', 'col')
- update: float32 [128, 512, 2048], P('owner', None, 'col')
The draws below stay inside these ranges and needn't reach their ends.
Inputs may be any that keep to these rules, and one draw needn't show every extreme that they name: `routing`: the row's expert as a local slot of the owner group that holds the row. `assignment`: a permutation: each expert is held in exactly one slot.
All inputs are finite; a program needn't handle non-finite values.
Results may differ from the reference program's by a relative error of at most 0.0065.
Values may be sent and summed in bfloat16 or wider, within the bound.
A program may use at most 64 MiB of HBM per device.

```python
import jax
import jax.numpy as jnp
from jax import lax

D = 2048
FFE = 512
EXP_DEV = 2
ROWS_DEV = 512
NS_ITERS = 2
EXPERTS = 128
ROWS = 32768


def draw_momentum(key, part):
    keys = jax.random.split(jax.random.fold_in(key, 11), 6)
    shape = (EXPERTS, FFE, D)
    row_scale = jnp.exp(jax.random.uniform(keys[0], (EXPERTS, FFE, 1), jnp.float32) * jnp.log(10.0))
    position = jnp.arange(D, dtype=jnp.float32) / D
    col_scale = jnp.exp(jax.random.uniform(keys[1], (1, 1, D), jnp.float32) * jnp.log(10.0) + jnp.log(3.0) * position[None, None, :])
    strengths = jnp.array([1.0, 0.7, 0.5], jnp.float32)
    left_factor = jnp.clip(jax.random.normal(keys[4], (EXPERTS, FFE, 3), jnp.float32), -4.0, 4.0)
    right_factor = jnp.clip(jax.random.normal(keys[5], (EXPERTS, 3, D), jnp.float32), -4.0, 4.0)
    noise = 1.08 * jnp.clip(jax.random.normal(keys[2], shape, jnp.float32), -5.0, 5.0)
    leading = jnp.einsum('efr,erd->efd', left_factor * strengths[None, None, :], right_factor, precision=lax.Precision.HIGHEST)
    mixed = jnp.clip(leading + noise, -6.0, 6.0)
    return 4.0 * mixed * row_scale * col_scale


def place_ends(values, stream_key, least, high):
    extent = values.shape
    spot = [jax.random.randint(jax.random.fold_in(stream_key, axis), (), 0, extent[axis]) for axis in range(len(extent))]
    values = values.at[tuple(spot)].set(least)
    longest = extent.index(max(extent))
    spot[longest] = (spot[longest] + 1) % extent[longest]
    return values.at[tuple(spot)].set(high)


def levels(own_key, shape, cuts, least, high):
    gain = 1.0
    for axis_at, blocks in cuts:
        draws = jax.random.uniform(jax.random.fold_in(jax.random.fold_in(own_key, 6), axis_at), (blocks,), jnp.float32, least / len(cuts), high / len(cuts))
        gain = gain * jnp.repeat(jnp.exp(draws), shape[axis_at] // blocks).reshape((-1,) + (1,) * (len(shape) - 1 - axis_at))
    return gain


def bell_draw(key, extent, spread, bound, cuts=(), kind=jnp.bfloat16):
    values = jax.random.normal(key, extent, jnp.float32) * spread
    if len(cuts) > 0:
        values = levels(key, extent, cuts, -0.22, 0.18) * values
    return jnp.clip(values, min=-bound, max=bound).astype(kind)


def setup_inputs(seed: int = 0) -> dict:
    seeds = jax.random.split(jax.random.key(seed), 6)
    momentum = draw_momentum(jax.random.fold_in(seeds[5], 71), 0)
    hidden_acts = bell_draw(seeds[1], (ROWS, FFE), 1.0, 6.0, ((0, 64),))
    output_grads = bell_draw(seeds[2], (ROWS, D), 1.0, 6.0, ((0, 64), (1, 4)))
    routing = place_ends(jax.random.randint(seeds[3], (ROWS,), 0, EXP_DEV), jax.random.fold_in(seeds[3], 1), 0, EXP_DEV - 1).astype(jnp.int32)
    assignment = jax.random.permutation(seeds[4], EXPERTS).astype(jnp.int32)
    return dict(momentum=momentum, hidden_acts=hidden_acts, output_grads=output_grads, routing=routing, assignment=assignment)


decay_rate = 0.95
epsilon = 1e-07
linear_weight = 3.4445
cubic_weight = -4.775
quintic_weight = 2.0315

def reference(momentum, hidden_acts, output_grads, routing, assignment):
    scaling = 0.2 * float(max(FFE, D)) ** 0.5

    def one_slot(slot_index):
        group_index = (slot_index // EXP_DEV).astype(jnp.int32)
        local_slot = (slot_index % EXP_DEV).astype(jnp.int32)
        first_row = (group_index * ROWS_DEV).astype(jnp.int32)
        hidden_rows = lax.dynamic_slice_in_dim(hidden_acts, first_row, ROWS_DEV, 0)
        grad_rows = lax.dynamic_slice_in_dim(output_grads, first_row, ROWS_DEV, 0)
        selected = lax.dynamic_slice_in_dim(routing, first_row, ROWS_DEV, 0) == local_slot
        masked = jnp.where(selected[:, None], grad_rows, jnp.zeros_like(grad_rows))
        gradient = jnp.dot(hidden_rows.T, masked, preferred_element_type=jnp.float32)
        expert = assignment[slot_index]
        updated = decay_rate * momentum[expert] + gradient
        squares = jnp.sum(updated * updated)
        iterate = (updated / (jnp.sqrt(squares) + epsilon)).astype(jnp.bfloat16)
        for turn_index in range(NS_ITERS):
            gram_matrix = jnp.dot(iterate, iterate.T, preferred_element_type=jnp.float32).astype(jnp.bfloat16)
            square = jnp.dot(gram_matrix, gram_matrix, preferred_element_type=jnp.float32)
            polynomial = (cubic_weight * gram_matrix.astype(jnp.float32) + quintic_weight * square).astype(jnp.bfloat16)
            product = jnp.dot(polynomial, iterate, preferred_element_type=jnp.float32)
            iterate = (linear_weight * iterate.astype(jnp.float32) + product).astype(jnp.bfloat16)
        return (updated, scaling * iterate.astype(jnp.float32))
    slots = jnp.arange(EXPERTS, dtype=jnp.int32)
    updated_all, update = lax.map(one_slot, slots)
    new_momentum = jnp.zeros_like(momentum).at[assignment].set(updated_all)
    return (new_momentum, update)
```

```python
import jax
import jax.numpy as jnp
from jax import lax
from jax.sharding import Mesh
from jax.sharding import PartitionSpec as P

D = 2048
FFE = 512
EXP_DEV = 2
OWNER = ("owner_0", "owner_1", "owner_2")

decay_rate = 0.95
epsilon = 1e-07
linear_weight = 3.4445
cubic_weight = -4.775
quintic_weight = 2.0315


def mm(a, b):
    return jnp.einsum(
        "jab,jbc->jac",
        a.astype(jnp.bfloat16),
        b.astype(jnp.bfloat16),
        preferred_element_type=jnp.float32,
    )


def body(momentum, hidden_acts, output_grads, routing, assignment):
    scaling = 0.2 * float(max(FFE, D)) ** 0.5
    n_col = lax.axis_size("col")
    order = assignment[:, None] == jnp.arange(assignment.shape[0], dtype=jnp.int32)[None, :]
    place = jnp.sum(
        jnp.where(order, jnp.arange(assignment.shape[0], dtype=jnp.int32)[:, None], 0), axis=0
    )
    ordered = momentum.at[assignment].get(mode="promise_in_bounds").astype(jnp.bfloat16)
    received = lax.all_to_all(ordered, OWNER, split_axis=0, concat_axis=1, tiled=True)
    slot_ids = jnp.arange(EXP_DEV, dtype=jnp.int32)
    selected = routing[:, None, None] == slot_ids[None, :, None]
    masked = jnp.where(selected, output_grads[:, None, :], jnp.zeros((), jnp.bfloat16))
    gradient = jnp.einsum("rf,rjd->jfd", hidden_acts, masked, preferred_element_type=jnp.float32)
    sent, _ = lax.optimization_barrier((gradient.astype(jnp.bfloat16), received))
    returned = lax.all_to_all(sent, OWNER, split_axis=1, concat_axis=0, tiled=True)
    updated = decay_rate * received.astype(jnp.float32) + gradient
    ub = updated.astype(jnp.bfloat16)
    partial = jnp.einsum("jfd,jgd->jfg", ub, ub, preferred_element_type=jnp.float32)
    pieces = lax.all_to_all(
        partial.astype(jnp.bfloat16).reshape(EXP_DEV, n_col, FFE // n_col, FFE),
        "col",
        split_axis=1,
        concat_axis=1,
        tiled=True,
    )
    piece = jnp.sum(pieces.astype(jnp.float32), axis=1).astype(jnp.bfloat16)
    full = lax.all_to_all(
        jnp.broadcast_to(piece[:, None], (EXP_DEV, n_col, FFE // n_col, FFE)),
        "col",
        split_axis=1,
        concat_axis=1,
        tiled=True,
    ).reshape(EXP_DEV, FFE, FFE)
    raw = full.astype(jnp.float32)
    eye = jnp.eye(FFE, dtype=jnp.bool_)[None]
    squares = jnp.sum(jnp.where(eye, raw, 0.0), axis=(1, 2), keepdims=True)
    inverse = 1.0 / (jnp.sqrt(squares) + epsilon)
    g1 = ((raw * inverse) * inverse).astype(jnp.bfloat16)
    p1 = (cubic_weight * g1.astype(jnp.float32) + quintic_weight * mm(g1, g1)).astype(jnp.bfloat16)
    t = mm(g1, p1)
    g2 = (
        linear_weight**2 * g1.astype(jnp.float32) + 2.0 * linear_weight * t + mm(p1, t)
    ).astype(jnp.bfloat16)
    p2 = (cubic_weight * g2.astype(jnp.float32) + quintic_weight * mm(g2, g2)).astype(jnp.bfloat16)
    rest = linear_weight * (p1.astype(jnp.float32) + p2.astype(jnp.float32)) + mm(p2, p1)
    update = (scaling * inverse) * (linear_weight**2 * updated + mm(rest, ub))
    back = returned.at[place].get(mode="promise_in_bounds")
    new_momentum = decay_rate * momentum + back.astype(jnp.float32)
    return (new_momentum, update)


def solution(mesh):
    torus = Mesh(
        mesh.devices.reshape(8, 4, 2, mesh.shape["col"]), ("owner_0", "owner_1", "owner_2", "col")
    )
    return jax.shard_map(
        body,
        mesh=torus,
        in_specs=(P(None, OWNER, "col"), P(OWNER, None), P(OWNER, "col"), P(OWNER), P()),
        out_specs=(P(None, OWNER, "col"), P(OWNER, None, "col")),
        check_vma=False,
    )
```

```python
import functools

import jax
import jax.numpy as jnp
from jax import lax
from jax.experimental import pallas as pl
from jax.experimental.pallas import tpu as pltpu
from jax.sharding import Mesh
from jax.sharding import PartitionSpec as P

OWNER = ("owner_0", "owner_1", "owner_2")
AXES = OWNER + ("col",)
MESH = pl.DeviceIdType.MESH

decay_rate = 0.95
epsilon = 1e-07
linear_weight = 3.4445
cubic_weight = -4.775
quintic_weight = 2.0315


def dot(a, b):
    return jnp.dot(a, b, preferred_element_type=jnp.float32)


def dot_rows(a, b):
    return lax.dot_general(a, b, (((1,), (1,)), ((), ())), preferred_element_type=jnp.float32)


def exchange_kernel(
    assign_ref,
    momentum_hbm,
    hidden_hbm,
    grads_hbm,
    routing_ref,
    back_hbm,
    update_hbm,
    mom,
    hid,
    out_grads,
    m_send,
    m_recv,
    g_send,
    upd32,
    ub,
    part,
    part_recv,
    whole_send,
    whole_recv,
    gram,
    poly,
    upd16,
    load_sem,
    own_sem,
    out_sem,
    m_ssem,
    m_rsem,
    g_ssem,
    g_rsem,
    p_ssem,
    p_rsem,
    w_ssem,
    w_rsem,
    *,
    sizes,
):
    nz, nx, nk, nc = sizes
    owners = nz * nx * nk
    rows = mom.shape[1]
    ffe = ub.shape[1]
    blk = ffe // nc
    z, x, k, c = (lax.axis_index(name) for name in AXES)
    me = (z * nx + x) * nk + k

    def peer(n):
        i = n % nz
        w = nx * nk - 1 - n // nz
        dz = nz // 2 + (i % 2) * ((i + 1) // 2) - (1 - i % 2) * (i // 2)
        pz = (z + dz) % nz
        px = (x + w // nk) % nx
        pk = (k + w % nk) % nk
        return (pz * nx + px) * nk + pk, (pz, px, pk, c)

    barrier = pltpu.get_barrier_semaphore()

    @pl.loop(0, owners - 1)
    def _(n):
        _, where = peer(n)
        pl.semaphore_signal(barrier, inc=1, device_id=where, device_id_type=MESH)

    for d in range(1, nc):
        pl.semaphore_signal(
            barrier, inc=1, device_id=(z, x, k, (c + d) % nc), device_id_type=MESH
        )

    loads = [
        pltpu.make_async_copy(momentum_hbm, mom, load_sem.at[0]),
        pltpu.make_async_copy(hidden_hbm, hid, load_sem.at[1]),
        pltpu.make_async_copy(grads_hbm, out_grads, load_sem.at[2]),
    ]
    for copy in loads:
        copy.start()
    loads[0].wait()
    for j in range(2):

        @pl.loop(0, owners, unroll=4)
        def _(o):
            m_send[j, o] = mom[assign_ref[2 * o + j]].astype(jnp.bfloat16)

    pl.semaphore_wait(barrier, owners - 1 + nc - 1)

    for j in range(2):

        @pl.loop(0, owners - 1)
        def _(n):
            to, where = peer(n)
            pltpu.make_async_remote_copy(
                src_ref=m_send.at[j, to],
                dst_ref=m_recv.at[j, me],
                send_sem=m_ssem.at[j],
                recv_sem=m_rsem.at[j],
                device_id=where,
                device_id_type=MESH,
            ).start()

    loads[1].wait()
    loads[2].wait()
    hid_t = hid[...].T
    for j in range(2):
        m_recv[j, me] = m_send[j, me]
        chosen = jnp.where(routing_ref[...] == j, hid_t, jnp.zeros((), jnp.bfloat16))
        upd32[j] = dot(chosen, out_grads[...])

        @pl.loop(0, owners, unroll=4)
        def _(o):
            at = pl.multiple_of(o * rows, rows)
            g_send[j, o] = upd32[j, pl.ds(at, rows), :].astype(jnp.bfloat16)

    own = []
    for j in range(2):
        copy = pltpu.make_async_copy(g_send.at[j, me], back_hbm.at[j, me], own_sem.at[j])
        copy.start()
        own.append(copy)

        @pl.loop(0, owners - 1)
        def _(n):
            to, where = peer(n)
            pltpu.make_async_remote_copy(
                src_ref=g_send.at[j, to],
                dst_ref=back_hbm.at[j, me],
                send_sem=g_ssem.at[j],
                recv_sem=g_rsem.at[j],
                device_id=where,
                device_id_type=MESH,
            ).start()

    def spread(source, target, send, recv, j):
        for d in range(1, nc):
            to = (c + d) % nc
            pltpu.make_async_remote_copy(
                src_ref=source(to),
                dst_ref=target,
                send_sem=send.at[j],
                recv_sem=recv.at[j],
                device_id=(z, x, k, to),
                device_id_type=MESH,
            ).start()

    def arrived(ref, sem):
        pltpu.make_async_copy(ref, ref, sem).wait()

    def partial_gram(j):
        arrived(m_recv.at[j, pl.ds(0, owners - 1)], m_rsem.at[j])

        @pl.loop(0, owners, unroll=4)
        def _(o):
            at = pl.multiple_of(o * rows, rows)
            upd32[j, pl.ds(at, rows), :] = decay_rate * m_recv[j, o].astype(
                jnp.float32
            ) + upd32[j, pl.ds(at, rows), :]

        ub[j] = upd32[j].astype(jnp.bfloat16)
        product = dot_rows(ub[j], ub[j])
        for b in range(nc):
            for t in range(3):
                at = (b + t) % nc * blk
                part[j, b, t] = product[b * blk : (b + 1) * blk, at : at + blk].astype(jnp.bfloat16)
        spread(lambda to: part.at[j, to], part_recv.at[j, c], p_ssem, p_rsem, j)
        part_recv[j, c] = part[j, c]

    def sum_parts(j):
        arrived(part_recv.at[j, pl.ds(0, nc - 1)], p_rsem.at[j])
        total = part_recv[j, 0].astype(jnp.float32)
        for b in range(1, nc):
            total = total + part_recv[j, b].astype(jnp.float32)
        whole_send[j] = total.astype(jnp.bfloat16)
        spread(lambda to: whole_send.at[j], whole_recv.at[j, c], w_ssem, w_rsem, j)
        whole_recv[j, c] = whole_send[j]

    partial_gram(0)
    sum_parts(0)
    partial_gram(1)

    @pl.loop(0, 2)
    def _(j):
        arrived(whole_recv.at[j, pl.ds(0, nc - 1)], w_rsem.at[j])
        eye = lax.broadcasted_iota(jnp.int32, (blk, blk), 0) == lax.broadcasted_iota(
            jnp.int32, (blk, blk), 1
        )
        diagonal = jnp.zeros((blk, blk), jnp.float32)
        for b in range(nc):
            diagonal = diagonal + jnp.where(eye, whole_recv[j, b, 0].astype(jnp.float32), 0.0)
        squares = jnp.sum(
            jnp.sum(diagonal, axis=0, keepdims=True), axis=1, keepdims=True
        )
        inverse = 1.0 / (jnp.sqrt(squares) + epsilon)
        for b in range(nc):
            for t in range(3):
                at = (b + t) % nc * blk
                block = (whole_recv[j, b, t].astype(jnp.float32) * inverse) * inverse
                gram[b * blk : (b + 1) * blk, at : at + blk] = block.astype(jnp.bfloat16)
                if t == 1:
                    gram[at : at + blk, b * blk : (b + 1) * blk] = block.T.astype(jnp.bfloat16)
        g1 = gram[...]
        p1 = (cubic_weight * g1.astype(jnp.float32) + quintic_weight * dot(g1, g1)).astype(
            jnp.bfloat16
        )
        poly[...] = p1
        t1 = dot(g1, p1)
        g2 = (
            linear_weight**2 * g1.astype(jnp.float32)
            + 2.0 * linear_weight * t1
            + dot(p1, t1.astype(jnp.bfloat16))
        ).astype(jnp.bfloat16)
        gram[...] = g2
        p2 = (cubic_weight * g2.astype(jnp.float32) + quintic_weight * dot(g2, g2)).astype(
            jnp.bfloat16
        )
        p1 = poly[...]
        rest = (
            linear_weight * (p1.astype(jnp.float32) + p2.astype(jnp.float32)) + dot(p2, p1)
        ).astype(jnp.bfloat16)
        upd16[j] = (
            inverse * (linear_weight**2 * upd32[j] + dot(rest, ub[j]))
        ).astype(jnp.bfloat16)
        pltpu.make_async_copy(upd16.at[j], update_hbm.at[j], out_sem.at[j]).start()

        @pl.when(j == 0)
        def _():
            sum_parts(1)

    for j in range(2):
        pltpu.make_async_copy(upd16.at[j], update_hbm.at[j], out_sem.at[j]).wait()
        arrived(m_send.at[j, pl.ds(0, owners - 1)], m_ssem.at[j])
        arrived(part.at[j, pl.ds(0, nc - 1)], p_ssem.at[j])
        arrived(whole_recv.at[j, pl.ds(0, nc - 1)], w_ssem.at[j])
        own[j].wait()
    for j in range(2):
        arrived(g_send.at[j, pl.ds(0, owners - 1)], g_ssem.at[j])
        arrived(back_hbm.at[j, pl.ds(0, owners - 1)], g_rsem.at[j])


def finish_kernel(
    assign_ref,
    momentum_hbm,
    back_hbm,
    update_hbm,
    new_hbm,
    out_hbm,
    mom,
    back,
    upd16,
    new,
    upd32,
    place,
    mom_sem,
    back_sem,
    upd_sem,
    new_sem,
    out_sem,
    *,
    scaling,
):
    experts = mom.shape[0]
    chunks = mom_sem.shape[0]
    step = experts // chunks
    owners = back.shape[1]
    back_copy = pltpu.make_async_copy(back_hbm, back, back_sem.at[0])
    back_copy.start()
    mom_copies, upd_copies, outs = [], [], []
    for q in range(chunks):
        part = pl.ds(q * step, step)
        copy = pltpu.make_async_copy(momentum_hbm.at[part], mom.at[part], mom_sem.at[q])
        copy.start()
        mom_copies.append(copy)
    for j in range(2):
        copy = pltpu.make_async_copy(update_hbm.at[j], upd16.at[j], upd_sem.at[j])
        copy.start()
        upd_copies.append(copy)

    @pl.loop(0, owners, unroll=4)
    def _(o):
        for j in range(2):
            place[assign_ref[2 * o + j]] = j * owners + o

    back_copy.wait()
    for q in range(chunks):
        mom_copies[q].wait()

        @pl.loop(q * step, (q + 1) * step, unroll=4)
        def _(e):
            at = place[e]
            new[e] = decay_rate * mom[e] + back[at // owners, at % owners].astype(jnp.float32)

        part = pl.ds(q * step, step)
        copy = pltpu.make_async_copy(new.at[part], new_hbm.at[part], new_sem.at[q])
        copy.start()
        outs.append(copy)
    for j in range(2):
        upd_copies[j].wait()
        upd32[j] = scaling * upd16[j].astype(jnp.float32)
        copy = pltpu.make_async_copy(upd32.at[j], out_hbm.at[j], out_sem.at[j])
        copy.start()
        outs.append(copy)
    for copy in outs:
        copy.wait()


def body(momentum, hidden_acts, output_grads, routing, assignment):
    sizes = tuple(lax.axis_size(name) for name in AXES)
    owners = sizes[0] * sizes[1] * sizes[2]
    nc = sizes[3]
    experts, rows, cols = momentum.shape
    tokens, ffe = hidden_acts.shape
    width = cols * nc
    blk = ffe // nc
    scaling = 0.2 * float(max(ffe, width)) ** 0.5
    bf16, f32 = jnp.bfloat16, jnp.float32
    anywhere = pl.BlockSpec(memory_space=pl.ANY)
    smem = pl.BlockSpec(memory_space=pltpu.SMEM)
    vmem = pl.BlockSpec(memory_space=pltpu.VMEM)
    sem = pltpu.SemaphoreType.DMA
    back, update = pl.pallas_call(
        functools.partial(exchange_kernel, sizes=sizes),
        out_shape=(
            jax.ShapeDtypeStruct((2, owners, rows, cols), bf16),
            jax.ShapeDtypeStruct((2, ffe, cols), bf16),
        ),
        in_specs=[smem, anywhere, anywhere, anywhere, vmem],
        out_specs=(anywhere, anywhere),
        scratch_shapes=[
            pltpu.VMEM((experts, rows, cols), f32),
            pltpu.VMEM((tokens, ffe), bf16),
            pltpu.VMEM((tokens, cols), bf16),
            pltpu.VMEM((2, owners, rows, cols), bf16),
            pltpu.VMEM((2, owners, rows, cols), bf16),
            pltpu.VMEM((2, owners, rows, cols), bf16),
            pltpu.VMEM((2, ffe, cols), f32),
            pltpu.VMEM((2, ffe, cols), bf16),
            pltpu.VMEM((2, nc, 3, blk, blk), bf16),
            pltpu.VMEM((2, nc, 3, blk, blk), bf16),
            pltpu.VMEM((2, 3, blk, blk), bf16),
            pltpu.VMEM((2, nc, 3, blk, blk), bf16),
            pltpu.VMEM((ffe, ffe), bf16),
            pltpu.VMEM((ffe, ffe), bf16),
            pltpu.VMEM((2, ffe, cols), bf16),
            sem((3,)),
            sem((2,)),
            sem((2,)),
            sem((2,)),
            sem((2,)),
            sem((2,)),
            sem((2,)),
            sem((2,)),
            sem((2,)),
            sem((2,)),
            sem((2,)),
        ],
        compiler_params=pltpu.CompilerParams(collective_id=0, has_side_effects=True),
        name="exchange",
    )(assignment, momentum, hidden_acts, output_grads, routing.reshape(1, tokens))
    chunks = 4
    return pl.pallas_call(
        functools.partial(finish_kernel, scaling=scaling),
        out_shape=(
            jax.ShapeDtypeStruct((experts, rows, cols), f32),
            jax.ShapeDtypeStruct((2, ffe, cols), f32),
        ),
        in_specs=[smem, anywhere, anywhere, anywhere],
        out_specs=(anywhere, anywhere),
        scratch_shapes=[
            pltpu.VMEM((experts, rows, cols), f32),
            pltpu.VMEM((2, owners, rows, cols), bf16),
            pltpu.VMEM((2, ffe, cols), bf16),
            pltpu.VMEM((experts, rows, cols), f32),
            pltpu.VMEM((2, ffe, cols), f32),
            pltpu.SMEM((experts,), jnp.int32),
            sem((chunks,)),
            sem((1,)),
            sem((2,)),
            sem((chunks,)),
            sem((2,)),
        ],
        name="finish",
    )(assignment, momentum, back, update)


def solution(mesh):
    owners = mesh.shape["owner"]
    cores = 2 if owners % 2 == 0 else 1
    across = 4 if owners % 8 == 0 else 1
    torus = Mesh(
        mesh.devices.reshape(owners // (across * cores), across, cores, mesh.shape["col"]), AXES
    )
    return jax.shard_map(
        body,
        mesh=torus,
        in_specs=(P(None, OWNER, "col"), P(OWNER, None), P(OWNER, "col"), P(OWNER), P()),
        out_specs=(P(None, OWNER, "col"), P(OWNER, None, "col")),
        check_vma=False,
    )
```

```python
import functools

import jax
import jax.numpy as jnp
from jax import lax
from jax.experimental import pallas as pl
from jax.experimental.pallas import tpu as pltpu
from jax.sharding import Mesh
from jax.sharding import PartitionSpec as P

OWNER = ("owner_0", "owner_1", "owner_2")
AXES = OWNER + ("col",)
MESH = pl.DeviceIdType.MESH

decay_rate = 0.95
epsilon = 1e-07
linear_weight = 3.4445
cubic_weight = -4.775
quintic_weight = 2.0315


def dot(a, b):
    return jnp.dot(a, b, preferred_element_type=jnp.float32)


def dot_rows(a, b):
    return lax.dot_general(a, b, (((1,), (1,)), ((), ())), preferred_element_type=jnp.float32)


def exchange_kernel(
    assign_ref,
    momentum_hbm,
    hidden_hbm,
    grads_hbm,
    routing_ref,
    new_ref,
    update_ref,
    mom,
    hid,
    out_grads,
    m_send,
    m_recv,
    g_send,
    g_recv,
    upd32,
    ub,
    part,
    part_recv,
    whole_send,
    whole_recv,
    gram,
    poly,
    load_sem,
    m_ssem,
    m_rsem,
    g_ssem,
    g_rsem,
    p_ssem,
    p_rsem,
    w_ssem,
    w_rsem,
    *,
    sizes,
    scaling,
):
    nz, nx, nk, nc = sizes
    owners = nz * nx * nk
    rows = mom.shape[1]
    ffe = ub.shape[1]
    blk = ffe // nc
    z, x, k, c = (lax.axis_index(name) for name in AXES)
    me = (z * nx + x) * nk + k

    def offsets(n):
        i = n % nz
        w = nx * nk - 1 - n // nz
        dz = nz // 2 + (i % 2) * ((i + 1) // 2) - (1 - i % 2) * (i // 2)
        return dz, w // nk, w % nk

    def peer(n):
        dz, dx, dk = offsets(n)
        pz, px, pk = (z + dz) % nz, (x + dx) % nx, (k + dk) % nk
        return (pz * nx + px) * nk + pk, (pz, px, pk, c)

    def sender(n):
        dz, dx, dk = offsets(n)
        return (((z + nz - dz) % nz) * nx + (x + nx - dx) % nx) * nk + (k + nk - dk) % nk

    barrier = pltpu.get_barrier_semaphore()

    @pl.loop(0, owners - 1)
    def _(n):
        _, where = peer(n)
        pl.semaphore_signal(barrier, inc=1, device_id=where, device_id_type=MESH)

    for d in range(1, nc):
        pl.semaphore_signal(
            barrier, inc=1, device_id=(z, x, k, (c + d) % nc), device_id_type=MESH
        )

    loads = [
        pltpu.make_async_copy(momentum_hbm, mom, load_sem.at[0]),
        pltpu.make_async_copy(hidden_hbm, hid, load_sem.at[1]),
        pltpu.make_async_copy(grads_hbm, out_grads, load_sem.at[2]),
    ]
    for copy in loads:
        copy.start()
    loads[0].wait()
    for j in range(2):

        @pl.loop(0, owners, unroll=4)
        def _(o):
            m_send[j, o] = mom[assign_ref[2 * o + j]].astype(jnp.bfloat16)

    pl.semaphore_wait(barrier, owners - 1 + nc - 1)

    for j in range(2):

        @pl.loop(0, owners - 1)
        def _(n):
            to, where = peer(n)
            pltpu.make_async_remote_copy(
                src_ref=m_send.at[j, to],
                dst_ref=m_recv.at[j, me],
                send_sem=m_ssem.at[j],
                recv_sem=m_rsem.at[j],
                device_id=where,
                device_id_type=MESH,
            ).start()

    loads[1].wait()
    loads[2].wait()
    hid_t = hid[...].T
    for j in range(2):
        m_recv[j, me] = m_send[j, me]
        chosen = jnp.where(routing_ref[...] == j, hid_t, jnp.zeros((), jnp.bfloat16))
        upd32[j] = dot(chosen, out_grads[...])

        @pl.loop(0, owners, unroll=4)
        def _(o):
            at = pl.multiple_of(o * rows, rows)
            g_send[o, j] = upd32[j, pl.ds(at, rows), :].astype(jnp.bfloat16)

    @pl.loop(0, owners - 1)
    def _(n):
        to, where = peer(n)
        pltpu.make_async_remote_copy(
            src_ref=g_send.at[to],
            dst_ref=g_recv.at[me],
            send_sem=g_ssem,
            recv_sem=g_rsem.at[n // nz],
            device_id=where,
            device_id_type=MESH,
        ).start()

    g_recv[me] = g_send[me]

    def spread(source, target, send, recv, j):
        for d in range(1, nc):
            to = (c + d) % nc
            pltpu.make_async_remote_copy(
                src_ref=source(to),
                dst_ref=target,
                send_sem=send.at[j],
                recv_sem=recv.at[j],
                device_id=(z, x, k, to),
                device_id_type=MESH,
            ).start()

    def arrived(ref, sem):
        pltpu.make_async_copy(ref, ref, sem).wait()

    def partial_gram(j):
        arrived(m_recv.at[j, pl.ds(0, owners - 1)], m_rsem.at[j])

        @pl.loop(0, owners, unroll=4)
        def _(o):
            at = pl.multiple_of(o * rows, rows)
            upd32[j, pl.ds(at, rows), :] = decay_rate * m_recv[j, o].astype(
                jnp.float32
            ) + upd32[j, pl.ds(at, rows), :]

        ub[j] = upd32[j].astype(jnp.bfloat16)
        product = dot_rows(ub[j], ub[j])
        for b in range(nc):
            for t in range(3):
                at = (b + t) % nc * blk
                part[j, b, t] = product[b * blk : (b + 1) * blk, at : at + blk].astype(jnp.bfloat16)
        spread(lambda to: part.at[j, to], part_recv.at[j, c], p_ssem, p_rsem, j)
        part_recv[j, c] = part[j, c]

    def sum_parts(j):
        arrived(part_recv.at[j, pl.ds(0, nc - 1)], p_rsem.at[j])
        total = part_recv[j, 0].astype(jnp.float32)
        for b in range(1, nc):
            total = total + part_recv[j, b].astype(jnp.float32)
        whole_send[j] = total.astype(jnp.bfloat16)
        spread(lambda to: whole_send.at[j], whole_recv.at[j, c], w_ssem, w_rsem, j)
        whole_recv[j, c] = whole_send[j]

    partial_gram(0)
    sum_parts(0)
    partial_gram(1)

    @pl.loop(0, 2)
    def _(j):
        arrived(whole_recv.at[j, pl.ds(0, nc - 1)], w_rsem.at[j])
        eye = lax.broadcasted_iota(jnp.int32, (blk, blk), 0) == lax.broadcasted_iota(
            jnp.int32, (blk, blk), 1
        )
        diagonal = jnp.zeros((blk, blk), jnp.float32)
        for b in range(nc):
            diagonal = diagonal + jnp.where(eye, whole_recv[j, b, 0].astype(jnp.float32), 0.0)
        squares = jnp.sum(
            jnp.sum(diagonal, axis=0, keepdims=True), axis=1, keepdims=True
        )
        inverse = 1.0 / (jnp.sqrt(squares) + epsilon)
        for b in range(nc):
            for t in range(3):
                at = (b + t) % nc * blk
                block = (whole_recv[j, b, t].astype(jnp.float32) * inverse) * inverse
                gram[b * blk : (b + 1) * blk, at : at + blk] = block.astype(jnp.bfloat16)
                if t == 1:
                    gram[at : at + blk, b * blk : (b + 1) * blk] = block.T.astype(jnp.bfloat16)
        g1 = gram[...]
        p1 = (cubic_weight * g1.astype(jnp.float32) + quintic_weight * dot(g1, g1)).astype(
            jnp.bfloat16
        )
        poly[...] = p1
        t1 = dot(g1, p1)
        g2 = (
            linear_weight**2 * g1.astype(jnp.float32)
            + 2.0 * linear_weight * t1
            + dot(p1, t1.astype(jnp.bfloat16))
        ).astype(jnp.bfloat16)
        gram[...] = g2
        p2 = (cubic_weight * g2.astype(jnp.float32) + quintic_weight * dot(g2, g2)).astype(
            jnp.bfloat16
        )
        p1 = poly[...]
        rest = (
            linear_weight * (p1.astype(jnp.float32) + p2.astype(jnp.float32)) + dot(p2, p1)
        ).astype(jnp.bfloat16)
        turned = (inverse * (linear_weight**2 * upd32[j] + dot(rest, ub[j]))).astype(jnp.bfloat16)
        update_ref[j] = scaling * turned.astype(jnp.float32)

        @pl.when(j == 0)
        def _():
            sum_parts(1)

    def combine(q):
        for i in range(nz):
            o = sender(q * nz + i)
            for j in range(2):
                new_ref[2 * o + j] = decay_rate * mom[assign_ref[2 * o + j]] + g_recv[o, j].astype(
                    jnp.float32
                )

    groups = owners // nz

    @pl.loop(0, groups - 1)
    def _(q):
        arrived(g_recv.at[pl.ds(0, nz)], g_rsem.at[q])
        combine(q)

    arrived(g_recv.at[pl.ds(0, nz - 1)], g_rsem.at[groups - 1])
    combine(groups - 1)

    for j in range(2):
        arrived(m_send.at[j, pl.ds(0, owners - 1)], m_ssem.at[j])
        arrived(part.at[j, pl.ds(0, nc - 1)], p_ssem.at[j])
        arrived(whole_recv.at[j, pl.ds(0, nc - 1)], w_ssem.at[j])
    arrived(g_send.at[pl.ds(0, owners - 1)], g_ssem)


def place_kernel(assign_ref, new_ref, update_ref, new_hbm, out_hbm, new_sem, out_sem):
    copy = pltpu.make_async_copy(update_ref, out_hbm, out_sem)
    copy.start()

    @pl.loop(0, new_ref.shape[0], unroll=8)
    def _(s):
        pltpu.make_async_copy(new_ref.at[s], new_hbm.at[assign_ref[s]], new_sem).start()

    copy.wait()
    pltpu.make_async_copy(new_ref, new_hbm, new_sem).wait()


def body(momentum, hidden_acts, output_grads, routing, assignment):
    sizes = tuple(lax.axis_size(name) for name in AXES)
    owners = sizes[0] * sizes[1] * sizes[2]
    nc = sizes[3]
    experts, rows, cols = momentum.shape
    tokens, ffe = hidden_acts.shape
    width = cols * nc
    blk = ffe // nc
    scaling = 0.2 * float(max(ffe, width)) ** 0.5
    bf16, f32 = jnp.bfloat16, jnp.float32
    hbm = pl.BlockSpec(memory_space=pltpu.HBM)
    smem = pl.BlockSpec(memory_space=pltpu.SMEM)
    vmem = pl.BlockSpec(memory_space=pltpu.VMEM)
    sem = pltpu.SemaphoreType.DMA
    placed, update = pl.pallas_call(
        functools.partial(exchange_kernel, sizes=sizes, scaling=scaling),
        out_shape=(
            pltpu.VMEM((experts, rows, cols), f32),
            pltpu.VMEM((2, ffe, cols), f32),
        ),
        in_specs=[smem, hbm, hbm, hbm, vmem],
        out_specs=(vmem, vmem),
        scratch_shapes=[
            pltpu.VMEM((experts, rows, cols), f32),
            pltpu.VMEM((tokens, ffe), bf16),
            pltpu.VMEM((tokens, cols), bf16),
            pltpu.VMEM((2, owners, rows, cols), bf16),
            pltpu.VMEM((2, owners, rows, cols), bf16),
            pltpu.VMEM((owners, 2, rows, cols), bf16),
            pltpu.VMEM((owners, 2, rows, cols), bf16),
            pltpu.VMEM((2, ffe, cols), f32),
            pltpu.VMEM((2, ffe, cols), bf16),
            pltpu.VMEM((2, nc, 3, blk, blk), bf16),
            pltpu.VMEM((2, nc, 3, blk, blk), bf16),
            pltpu.VMEM((2, 3, blk, blk), bf16),
            pltpu.VMEM((2, nc, 3, blk, blk), bf16),
            pltpu.VMEM((ffe, ffe), bf16),
            pltpu.VMEM((ffe, ffe), bf16),
            sem((3,)),
            sem((2,)),
            sem((2,)),
            sem(()),
            sem((owners // sizes[0],)),
            sem((2,)),
            sem((2,)),
            sem((2,)),
            sem((2,)),
        ],
        compiler_params=pltpu.CompilerParams(
            collective_id=0, has_side_effects=True, vmem_limit_bytes=36 << 20
        ),
        name="exchange",
    )(
        pltpu.with_memory_space_constraint(assignment, pltpu.HBM),
        pltpu.with_memory_space_constraint(momentum, pltpu.HBM),
        pltpu.with_memory_space_constraint(hidden_acts, pltpu.HBM),
        pltpu.with_memory_space_constraint(output_grads, pltpu.HBM),
        pltpu.with_memory_space_constraint(routing.reshape(1, tokens), pltpu.HBM),
    )
    return pl.pallas_call(
        place_kernel,
        out_shape=(
            jax.ShapeDtypeStruct((experts, rows, cols), f32),
            jax.ShapeDtypeStruct((2, ffe, cols), f32),
        ),
        in_specs=[smem, vmem, vmem],
        out_specs=(hbm, hbm),
        scratch_shapes=[sem(()), sem(())],
        compiler_params=pltpu.CompilerParams(vmem_limit_bytes=4 << 20),
        name="place",
    )(
        assignment,
        pltpu.with_memory_space_constraint(placed, pltpu.VMEM),
        pltpu.with_memory_space_constraint(update, pltpu.VMEM),
    )


def solution(mesh):
    owners = mesh.shape["owner"]
    cores = 2 if owners % 2 == 0 else 1
    across = 4 if owners % 8 == 0 else 1
    torus = Mesh(
        mesh.devices.reshape(owners // (across * cores), across, cores, mesh.shape["col"]), AXES
    )
    return jax.shard_map(
        body,
        mesh=torus,
        in_specs=(P(None, OWNER, "col"), P(OWNER, None), P(OWNER, "col"), P(OWNER), P()),
        out_specs=(P(None, OWNER, "col"), P(OWNER, None, "col")),
        check_vma=False,
    )
```

```python
import functools

import jax
import jax.numpy as jnp
from jax import lax
from jax.experimental import pallas as pl
from jax.experimental.pallas import tpu as pltpu
from jax.sharding import Mesh
from jax.sharding import PartitionSpec as P

OWNER = ("owner_0", "owner_1", "owner_2")
AXES = OWNER + ("col",)
MESH = pl.DeviceIdType.MESH

decay_rate = 0.95
epsilon = 1e-07
linear_weight = 3.4445
cubic_weight = -4.775
quintic_weight = 2.0315


def dot(a, b):
    return jnp.dot(a, b, preferred_element_type=jnp.float32)


def dot_rows(a, b):
    return lax.dot_general(a, b, (((1,), (1,)), ((), ())), preferred_element_type=jnp.float32)


def exchange_kernel(
    assign_ref,
    momentum_hbm,
    hidden_hbm,
    grads_hbm,
    routing_ref,
    new_ref,
    update_ref,
    mom,
    hid,
    out_grads,
    m_send,
    m_recv,
    g_send,
    g_recv,
    upd32,
    ub,
    part,
    part_recv,
    whole_send,
    whole_recv,
    gram,
    poly,
    hop_sem,
    load_sem,
    m_ssem,
    m_rsem,
    g_ssem,
    g_rsem,
    p_ssem,
    p_rsem,
    w_ssem,
    w_rsem,
    *,
    sizes,
    scaling,
):
    nz, nx, nk, nc = sizes
    owners = nz * nx * nk
    rows = mom.shape[1]
    ffe = ub.shape[1]
    blk = ffe // nc
    z, x, k, c = (lax.axis_index(name) for name in AXES)
    me = (z * nx + x) * nk + k

    def offsets(n):
        i = n % nz
        w = nx * nk - 1 - n // nz
        dz = nz // 2 + (i % 2) * ((i + 1) // 2) - (1 - i % 2) * (i // 2)
        return dz, w // nk, w % nk

    def peer(n):
        dz, dx, dk = offsets(n)
        pz, px, pk = (z + dz) % nz, (x + dx) % nx, (k + dk) % nk
        return (pz * nx + px) * nk + pk, (pz, px, pk, c)

    def sender(n):
        dz, dx, dk = offsets(n)
        return (((z + nz - dz) % nz) * nx + (x + nx - dx) % nx) * nk + (k + nk - dk) % nk

    zs = [lax.rem(z + d, nz) for d in range(nz)]
    xs = [lax.rem(x + d, nx) for d in range(nx)]
    ks = [lax.rem(k + d, nk) for d in range(nk)]
    above, below = (zs[1], x, k, c), (zs[nz - 1], x, k, c)
    barrier = pltpu.get_barrier_semaphore()
    for dx in sorted(range(nx), key=lambda d: -min(d, nx - d)):
        for dk in range(nk - 1, -1, -1):
            for dz in (1, nz - 1, 0):
                if (dz, dx, dk) != (0, 0, 0):
                    pl.semaphore_signal(
                        barrier,
                        inc=1,
                        device_id=(zs[dz], xs[dx], ks[dk], c),
                        device_id_type=MESH,
                    )
    for d in range(1, nc):
        pl.semaphore_signal(
            barrier, inc=1, device_id=(z, x, k, lax.rem(c + d, nc)), device_id_type=MESH
        )

    loads = [
        pltpu.make_async_copy(momentum_hbm, mom, load_sem.at[0]),
        pltpu.make_async_copy(hidden_hbm, hid, load_sem.at[1]),
        pltpu.make_async_copy(grads_hbm, out_grads, load_sem.at[2]),
    ]
    for copy in loads:
        copy.start()
    loads[0].wait()
    def convert(j):
        @pl.loop(0, owners, unroll=4)
        def _(o):
            m_send[j, o] = mom[assign_ref[2 * o + j]].astype(jnp.bfloat16)

    def send_planes(j, planes, first=0):
        @pl.loop(first, nx * nk)
        def _(w):
            px, pk = lax.rem(x + w // nk, nx), lax.rem(k + w % nk, nk)
            for dz in planes:
                pltpu.make_async_remote_copy(
                    src_ref=m_send.at[j, (zs[dz] * nx + px) * nk + pk],
                    dst_ref=m_recv.at[j, me],
                    send_sem=m_ssem.at[j],
                    recv_sem=m_rsem.at[j],
                    device_id=(zs[dz], px, pk, c),
                    device_id_type=MESH,
                ).start()

    convert(0)
    pl.semaphore_wait(barrier, 3 * nx * nk - 1 + nc - 1)
    half = nz // 2
    for d in range(1, half + 1):
        if d > 1:
            pl.semaphore_wait(hop_sem.at[d - 2], 2)
        if d < half:
            for where in (above, below):
                pl.semaphore_signal(
                    hop_sem.at[d - 1], inc=1, device_id=where, device_id_type=MESH
                )
        send_planes(0, [d] if d == half else [d, nz - d])
    send_planes(0, [0], 1)
    convert(1)
    order = [half]
    for d in range(half - 1, 0, -1):
        order += [nz - d, d]
    send_planes(1, order)
    send_planes(1, [0], 1)

    loads[1].wait()
    loads[2].wait()
    hid_t = hid[...].T
    for j in range(2):
        m_recv[j, me] = m_send[j, me]
        chosen = jnp.where(routing_ref[...] == j, hid_t, jnp.zeros((), jnp.bfloat16))
        upd32[j] = dot(chosen, out_grads[...])

        @pl.loop(0, owners, unroll=4)
        def _(o):
            at = pl.multiple_of(o * rows, rows)
            g_send[o, j] = upd32[j, pl.ds(at, rows), :].astype(jnp.bfloat16)

    @pl.loop(0, owners - 1)
    def _(n):
        to, where = peer(n)
        pltpu.make_async_remote_copy(
            src_ref=g_send.at[to],
            dst_ref=g_recv.at[me],
            send_sem=g_ssem,
            recv_sem=g_rsem.at[n // nz],
            device_id=where,
            device_id_type=MESH,
        ).start()

    g_recv[me] = g_send[me]

    def spread(source, target, send, recv, j):
        for d in range(1, nc):
            to = (c + d) % nc
            pltpu.make_async_remote_copy(
                src_ref=source(to),
                dst_ref=target,
                send_sem=send.at[j],
                recv_sem=recv.at[j],
                device_id=(z, x, k, to),
                device_id_type=MESH,
            ).start()

    def arrived(ref, sem):
        pltpu.make_async_copy(ref, ref, sem).wait()

    def partial_gram(j):
        arrived(m_recv.at[j, pl.ds(0, owners - 1)], m_rsem.at[j])

        @pl.loop(0, owners, unroll=4)
        def _(o):
            at = pl.multiple_of(o * rows, rows)
            upd32[j, pl.ds(at, rows), :] = decay_rate * m_recv[j, o].astype(
                jnp.float32
            ) + upd32[j, pl.ds(at, rows), :]

        ub[j] = upd32[j].astype(jnp.bfloat16)
        product = dot_rows(ub[j], ub[j])
        for b in range(nc):
            for t in range(3):
                at = (b + t) % nc * blk
                part[j, b, t] = product[b * blk : (b + 1) * blk, at : at + blk].astype(jnp.bfloat16)
        spread(lambda to: part.at[j, to], part_recv.at[j, c], p_ssem, p_rsem, j)
        part_recv[j, c] = part[j, c]

    def sum_parts(j):
        arrived(part_recv.at[j, pl.ds(0, nc - 1)], p_rsem.at[j])
        total = part_recv[j, 0].astype(jnp.float32)
        for b in range(1, nc):
            total = total + part_recv[j, b].astype(jnp.float32)
        whole_send[j] = total.astype(jnp.bfloat16)
        spread(lambda to: whole_send.at[j], whole_recv.at[j, c], w_ssem, w_rsem, j)
        whole_recv[j, c] = whole_send[j]

    partial_gram(0)
    sum_parts(0)
    partial_gram(1)

    @pl.loop(0, 2)
    def _(j):
        arrived(whole_recv.at[j, pl.ds(0, nc - 1)], w_rsem.at[j])
        eye = lax.broadcasted_iota(jnp.int32, (blk, blk), 0) == lax.broadcasted_iota(
            jnp.int32, (blk, blk), 1
        )
        diagonal = jnp.zeros((blk, blk), jnp.float32)
        for b in range(nc):
            diagonal = diagonal + jnp.where(eye, whole_recv[j, b, 0].astype(jnp.float32), 0.0)
        squares = jnp.sum(
            jnp.sum(diagonal, axis=0, keepdims=True), axis=1, keepdims=True
        )
        inverse = 1.0 / (jnp.sqrt(squares) + epsilon)
        for b in range(nc):
            for t in range(3):
                at = (b + t) % nc * blk
                block = (whole_recv[j, b, t].astype(jnp.float32) * inverse) * inverse
                gram[b * blk : (b + 1) * blk, at : at + blk] = block.astype(jnp.bfloat16)
                if t == 1:
                    gram[at : at + blk, b * blk : (b + 1) * blk] = block.T.astype(jnp.bfloat16)
        g1 = gram[...]
        p1 = (cubic_weight * g1.astype(jnp.float32) + quintic_weight * dot(g1, g1)).astype(
            jnp.bfloat16
        )
        poly[...] = p1
        t1 = dot(g1, p1)
        g2 = (
            linear_weight**2 * g1.astype(jnp.float32)
            + 2.0 * linear_weight * t1
            + dot(p1, t1.astype(jnp.bfloat16))
        ).astype(jnp.bfloat16)
        gram[...] = g2
        p2 = (cubic_weight * g2.astype(jnp.float32) + quintic_weight * dot(g2, g2)).astype(
            jnp.bfloat16
        )
        p1 = poly[...]
        rest = (
            linear_weight * (p1.astype(jnp.float32) + p2.astype(jnp.float32)) + dot(p2, p1)
        ).astype(jnp.bfloat16)
        turned = (inverse * (linear_weight**2 * upd32[j] + dot(rest, ub[j]))).astype(jnp.bfloat16)
        update_ref[j] = scaling * turned.astype(jnp.float32)

        @pl.when(j == 0)
        def _():
            sum_parts(1)

    def combine(q):
        for i in range(nz):
            o = sender(q * nz + i)
            for j in range(2):
                new_ref[2 * o + j] = decay_rate * mom[assign_ref[2 * o + j]] + g_recv[o, j].astype(
                    jnp.float32
                )

    groups = owners // nz

    @pl.loop(0, groups - 1)
    def _(q):
        arrived(g_recv.at[pl.ds(0, nz)], g_rsem.at[q])
        combine(q)

    arrived(g_recv.at[pl.ds(0, nz - 1)], g_rsem.at[groups - 1])
    combine(groups - 1)

    for j in range(2):
        arrived(m_send.at[j, pl.ds(0, owners - 1)], m_ssem.at[j])
        arrived(part.at[j, pl.ds(0, nc - 1)], p_ssem.at[j])
        arrived(whole_recv.at[j, pl.ds(0, nc - 1)], w_ssem.at[j])
    arrived(g_send.at[pl.ds(0, owners - 1)], g_ssem)


def place_kernel(assign_ref, new_ref, update_ref, new_hbm, out_hbm, new_sem, out_sem):
    copy = pltpu.make_async_copy(update_ref, out_hbm, out_sem)
    copy.start()

    @pl.loop(0, new_ref.shape[0], unroll=8)
    def _(s):
        pltpu.make_async_copy(new_ref.at[s], new_hbm.at[assign_ref[s]], new_sem).start()

    copy.wait()
    pltpu.make_async_copy(new_ref, new_hbm, new_sem).wait()


def body(momentum, hidden_acts, output_grads, routing, assignment):
    sizes = tuple(lax.axis_size(name) for name in AXES)
    owners = sizes[0] * sizes[1] * sizes[2]
    nc = sizes[3]
    experts, rows, cols = momentum.shape
    tokens, ffe = hidden_acts.shape
    width = cols * nc
    blk = ffe // nc
    scaling = 0.2 * float(max(ffe, width)) ** 0.5
    bf16, f32 = jnp.bfloat16, jnp.float32
    hbm = pl.BlockSpec(memory_space=pltpu.HBM)
    smem = pl.BlockSpec(memory_space=pltpu.SMEM)
    vmem = pl.BlockSpec(memory_space=pltpu.VMEM)
    sem = pltpu.SemaphoreType.DMA
    placed, update = pl.pallas_call(
        functools.partial(exchange_kernel, sizes=sizes, scaling=scaling),
        out_shape=(
            pltpu.VMEM((experts, rows, cols), f32),
            pltpu.VMEM((2, ffe, cols), f32),
        ),
        in_specs=[smem, hbm, hbm, hbm, vmem],
        out_specs=(vmem, vmem),
        scratch_shapes=[
            pltpu.VMEM((experts, rows, cols), f32),
            pltpu.VMEM((tokens, ffe), bf16),
            pltpu.VMEM((tokens, cols), bf16),
            pltpu.VMEM((2, owners, rows, cols), bf16),
            pltpu.VMEM((2, owners, rows, cols), bf16),
            pltpu.VMEM((owners, 2, rows, cols), bf16),
            pltpu.VMEM((owners, 2, rows, cols), bf16),
            pltpu.VMEM((2, ffe, cols), f32),
            pltpu.VMEM((2, ffe, cols), bf16),
            pltpu.VMEM((2, nc, 3, blk, blk), bf16),
            pltpu.VMEM((2, nc, 3, blk, blk), bf16),
            pltpu.VMEM((2, 3, blk, blk), bf16),
            pltpu.VMEM((2, nc, 3, blk, blk), bf16),
            pltpu.VMEM((ffe, ffe), bf16),
            pltpu.VMEM((ffe, ffe), bf16),
            pltpu.SemaphoreType.REGULAR((sizes[0] // 2 - 1,)),
            sem((3,)),
            sem((2,)),
            sem((2,)),
            sem(()),
            sem((owners // sizes[0],)),
            sem((2,)),
            sem((2,)),
            sem((2,)),
            sem((2,)),
        ],
        compiler_params=pltpu.CompilerParams(
            collective_id=0, has_side_effects=True, vmem_limit_bytes=36 << 20
        ),
        name="exchange",
    )(
        pltpu.with_memory_space_constraint(assignment, pltpu.HBM),
        pltpu.with_memory_space_constraint(momentum, pltpu.HBM),
        pltpu.with_memory_space_constraint(hidden_acts, pltpu.HBM),
        pltpu.with_memory_space_constraint(output_grads, pltpu.HBM),
        pltpu.with_memory_space_constraint(routing.reshape(1, tokens), pltpu.HBM),
    )
    return pl.pallas_call(
        place_kernel,
        out_shape=(
            jax.ShapeDtypeStruct((experts, rows, cols), f32),
            jax.ShapeDtypeStruct((2, ffe, cols), f32),
        ),
        in_specs=[smem, vmem, vmem],
        out_specs=(hbm, hbm),
        scratch_shapes=[sem(()), sem(())],
        compiler_params=pltpu.CompilerParams(vmem_limit_bytes=4 << 20),
        name="place",
    )(
        assignment,
        pltpu.with_memory_space_constraint(placed, pltpu.VMEM),
        pltpu.with_memory_space_constraint(update, pltpu.VMEM),
    )


def solution(mesh):
    owners = mesh.shape["owner"]
    cores = 2 if owners % 2 == 0 else 1
    across = 4 if owners % 8 == 0 else 1
    torus = Mesh(
        mesh.devices.reshape(owners // (across * cores), across, cores, mesh.shape["col"]), AXES
    )
    return jax.shard_map(
        body,
        mesh=torus,
        in_specs=(P(None, OWNER, "col"), P(OWNER, None), P(OWNER, "col"), P(OWNER), P()),
        out_specs=(P(None, OWNER, "col"), P(OWNER, None, "col")),
        check_vma=False,
    )
```

```python
import functools

import jax
import jax.numpy as jnp
from jax import lax
from jax.experimental import pallas as pl
from jax.experimental.pallas import tpu as pltpu
from jax.sharding import Mesh
from jax.sharding import PartitionSpec as P

OWNER = ("owner_0", "owner_1", "owner_2")
AXES = OWNER + ("col",)
MESH = pl.DeviceIdType.MESH

decay_rate = 0.95
epsilon = 1e-07
linear_weight = 3.4445
cubic_weight = -4.775
quintic_weight = 2.0315


def dot(a, b):
    return jnp.dot(a, b, preferred_element_type=jnp.float32)


def dot_rows(a, b):
    return lax.dot_general(a, b, (((1,), (1,)), ((), ())), preferred_element_type=jnp.float32)


def exchange_kernel(
    assign_hbm,
    momentum_hbm,
    hidden_hbm,
    grads_hbm,
    routing_hbm,
    new_ref,
    update_ref,
    assign_ref,
    routing_ref,
    mom,
    hid,
    out_grads,
    m_send,
    m_recv,
    g_send,
    g_recv,
    upd32,
    ub,
    part,
    part_recv,
    whole_send,
    whole_recv,
    gram,
    poly,
    hop_sem,
    load_sem,
    m_ssem,
    m_rsem,
    g_ssem,
    g_rsem,
    p_ssem,
    p_rsem,
    w_ssem,
    w_rsem,
    *,
    sizes,
    scaling,
):
    nz, nx, nk, nc = sizes
    owners = nz * nx * nk
    rows = mom.shape[1]
    ffe = ub.shape[1]
    blk = ffe // nc
    z, x, k, c = (lax.axis_index(name) for name in AXES)
    me = (z * nx + x) * nk + k

    def offsets(n):
        i = n % nz
        w = nx * nk - 1 - n // nz
        dz = nz // 2 + (i % 2) * ((i + 1) // 2) - (1 - i % 2) * (i // 2)
        return dz, w // nk, w % nk

    def sender(n):
        dz, dx, dk = offsets(n)
        return (((z + nz - dz) % nz) * nx + (x + nx - dx) % nx) * nk + (k + nk - dk) % nk

    zs = [lax.rem(z + d, nz) for d in range(nz)]
    xs = [lax.rem(x + d, nx) for d in range(nx)]
    ks = [lax.rem(k + d, nk) for d in range(nk)]
    above, below = (zs[1], x, k, c), (zs[nz - 1], x, k, c)
    barrier = pltpu.get_barrier_semaphore()
    for dx in sorted(range(nx), key=lambda d: -min(d, nx - d)):
        for dk in range(nk - 1, -1, -1):
            for dz in (1, nz - 1, 0):
                if (dz, dx, dk) != (0, 0, 0):
                    pl.semaphore_signal(
                        barrier,
                        inc=1,
                        device_id=(zs[dz], xs[dx], ks[dk], c),
                        device_id_type=MESH,
                    )
    for d in range(1, nc):
        pl.semaphore_signal(
            barrier, inc=1, device_id=(z, x, k, lax.rem(c + d, nc)), device_id_type=MESH
        )

    pairs = (
        (assign_hbm, assign_ref),
        (momentum_hbm, mom),
        (hidden_hbm, hid),
        (grads_hbm, out_grads),
        (routing_hbm, routing_ref),
    )
    loads = [
        pltpu.make_async_copy(source, target, load_sem.at[i])
        for i, (source, target) in enumerate(pairs)
    ]
    for copy in loads:
        copy.start()
    loads[0].wait()
    loads[1].wait()
    def convert(j):
        @pl.loop(0, owners, unroll=4)
        def _(o):
            m_send[j, o] = mom[assign_ref[2 * o + j]].astype(jnp.bfloat16)

    def send_planes(j, planes, first=0):
        @pl.loop(first, nx * nk)
        def _(w):
            px, pk = lax.rem(x + w // nk, nx), lax.rem(k + w % nk, nk)
            for dz in planes:
                pltpu.make_async_remote_copy(
                    src_ref=m_send.at[j, (zs[dz] * nx + px) * nk + pk],
                    dst_ref=m_recv.at[j, me],
                    send_sem=m_ssem.at[j],
                    recv_sem=m_rsem.at[j],
                    device_id=(zs[dz], px, pk, c),
                    device_id_type=MESH,
                ).start()

    convert(0)
    pl.semaphore_wait(barrier, 3 * nx * nk - 1 + nc - 1)
    half = nz // 2
    for d in range(1, half + 1):
        if d > 1:
            pl.semaphore_wait(hop_sem.at[d - 2], 2)
        if d < half:
            for where in (above, below):
                pl.semaphore_signal(
                    hop_sem.at[d - 1], inc=1, device_id=where, device_id_type=MESH
                )
        send_planes(0, [d] if d == half else [d, nz - d])
    send_planes(0, [0], 1)
    convert(1)
    def paced(alpha, send):
        late = [1 - alpha * max(0.0, 1 - p / half) for p in range(nz)]
        turn = [(p % 2) * half + p // 2 for p in range(nz)]
        jobs = [(i, p) for i in range(nx * nk) for p in turn]
        for i, p in sorted(jobs, key=lambda job: (job[0] + 1) * late[job[1]]):
            w = nx * nk - 1 - i
            px, pk = xs[w // nk], ks[w % nk]

            def go(p=p, i=i, px=px, pk=pk):
                send(i, (p * nx + px) * nk + pk, (p, px, pk, c))

            if w > 0:
                go()
            else:
                pl.when(z != p)(go)

    def send_second(i, to, where):
        pltpu.make_async_remote_copy(
            src_ref=m_send.at[1, to],
            dst_ref=m_recv.at[1, me],
            send_sem=m_ssem.at[1],
            recv_sem=m_rsem.at[1],
            device_id=where,
            device_id_type=MESH,
        ).start()

    paced(0.1, send_second)

    for copy in loads[2:]:
        copy.wait()
    hid_t = hid[...].T
    for j in range(2):
        m_recv[j, me] = m_send[j, me]
        chosen = jnp.where(routing_ref[...] == j, hid_t, jnp.zeros((), jnp.bfloat16))
        upd32[j] = dot(chosen, out_grads[...])

        @pl.loop(0, owners, unroll=4)
        def _(o):
            at = pl.multiple_of(o * rows, rows)
            g_send[o, j] = upd32[j, pl.ds(at, rows), :].astype(jnp.bfloat16)

    def send_back(i, to, where):
        pltpu.make_async_remote_copy(
            src_ref=g_send.at[to],
            dst_ref=g_recv.at[me],
            send_sem=g_ssem,
            recv_sem=g_rsem.at[i],
            device_id=where,
            device_id_type=MESH,
        ).start()

    paced(0.2, send_back)

    g_recv[me] = g_send[me]

    depth = part.shape[2] // 2

    def spread(source, target, send, recv, j, h):
        for d in (2, 1, 3):
            to = lax.rem(c + d, nc)
            pltpu.make_async_remote_copy(
                src_ref=source(to),
                dst_ref=target,
                send_sem=send.at[j],
                recv_sem=recv.at[j, h],
                device_id=(z, x, k, to),
                device_id_type=MESH,
            ).start()

    def arrived(ref, sem):
        pltpu.make_async_copy(ref, ref, sem).wait()

    def partial_gram(j):
        arrived(m_recv.at[j, pl.ds(0, owners - 1)], m_rsem.at[j])

        @pl.loop(0, owners, unroll=4)
        def _(o):
            at = pl.multiple_of(o * rows, rows)
            upd32[j, pl.ds(at, rows), :] = decay_rate * m_recv[j, o].astype(
                jnp.float32
            ) + upd32[j, pl.ds(at, rows), :]

        ub[j] = upd32[j].astype(jnp.bfloat16)
        product = dot_rows(ub[j], ub[j])
        product = product.astype(jnp.bfloat16)
        for b in range(nc):
            own = product[b * blk : (b + 1) * blk]
            after = (b + 1) % nc * blk
            top, left = b % 2 * blk + b // 2 * (blk // 2), (b % 2 + 2) * blk
            part[j, b, 0:blk] = own[:, b * blk : (b + 1) * blk]
            part[j, b, blk : 2 * blk] = own[:, after : after + blk]
            part[j, b, 2 * blk :] = product[top : top + blk // 2, left : left + blk]
        for h in range(2):
            piece = pl.ds(h * depth, depth)
            spread(
                lambda to: part.at[j, to, piece], part_recv.at[j, c, piece], p_ssem, p_rsem, j, h
            )
        part_recv[j, c] = part[j, c]

    def sum_parts(j):
        for h in range(2):
            piece = pl.ds(h * depth, depth)
            arrived(part_recv.at[j, pl.ds(0, nc - 1), piece], p_rsem.at[j, h])
            total = part_recv[j, 0, piece].astype(jnp.float32)
            for b in range(1, nc):
                total = total + part_recv[j, b, piece].astype(jnp.float32)
            whole_send[j, piece] = total.astype(jnp.bfloat16)
            spread(
                lambda to: whole_send.at[j, piece],
                whole_recv.at[j, c, piece],
                w_ssem,
                w_rsem,
                j,
                h,
            )
        whole_recv[j, c] = whole_send[j]

    partial_gram(0)
    sum_parts(0)
    partial_gram(1)
    sum_parts(1)

    @pl.loop(0, 2)
    def _(j):
        for h in range(2):
            piece = pl.ds(h * depth, depth)
            arrived(whole_recv.at[j, pl.ds(0, nc - 1), piece], w_rsem.at[j, h])
        eye = lax.broadcasted_iota(jnp.int32, (blk, blk), 0) == lax.broadcasted_iota(
            jnp.int32, (blk, blk), 1
        )
        diagonal = jnp.zeros((blk, blk), jnp.float32)
        for b in range(nc):
            diagonal = diagonal + jnp.where(
                eye, whole_recv[j, b, 0:blk].astype(jnp.float32), 0.0
            )
        squares = jnp.sum(
            jnp.sum(diagonal, axis=0, keepdims=True), axis=1, keepdims=True
        )
        inverse = 1.0 / (jnp.sqrt(squares) + epsilon)

        def scaled(*where):
            return (whole_recv[where].astype(jnp.float32) * inverse) * inverse

        def fill(p, q, block):
            gram[p * blk : (p + 1) * blk, q * blk : (q + 1) * blk] = block.astype(jnp.bfloat16)
            if p != q:
                gram[q * blk : (q + 1) * blk, p * blk : (p + 1) * blk] = block.T.astype(
                    jnp.bfloat16
                )

        for b in range(nc):
            fill(b, b, scaled(j, b, slice(0, blk)))
            fill(b, (b + 1) % nc, scaled(j, b, slice(blk, 2 * blk)))
            if b < 2:
                rest = slice(2 * blk, None)
                fill(b, b + 2, jnp.concatenate([scaled(j, b, rest), scaled(j, b + 2, rest)], 0))
        g1 = gram[...]
        p1 = (cubic_weight * g1.astype(jnp.float32) + quintic_weight * dot(g1, g1)).astype(
            jnp.bfloat16
        )
        poly[...] = p1
        t1 = dot(g1, p1)
        g2 = (
            linear_weight**2 * g1.astype(jnp.float32)
            + 2.0 * linear_weight * t1
            + dot(p1, t1.astype(jnp.bfloat16))
        ).astype(jnp.bfloat16)
        gram[...] = g2
        p2 = (cubic_weight * g2.astype(jnp.float32) + quintic_weight * dot(g2, g2)).astype(
            jnp.bfloat16
        )
        p1 = poly[...]
        rest = (
            linear_weight * (p1.astype(jnp.float32) + p2.astype(jnp.float32)) + dot(p2, p1)
        ).astype(jnp.bfloat16)
        turned = (inverse * (linear_weight**2 * upd32[j] + dot(rest, ub[j]))).astype(jnp.bfloat16)
        update_ref[j] = scaling * turned.astype(jnp.float32)

    def combine(q):
        for i in range(nz):
            o = sender(q * nz + i)
            for j in range(2):
                new_ref[2 * o + j] = decay_rate * mom[assign_ref[2 * o + j]] + g_recv[o, j].astype(
                    jnp.float32
                )

    groups = owners // nz

    @pl.loop(0, groups - 1)
    def _(q):
        arrived(g_recv.at[pl.ds(0, nz)], g_rsem.at[q])
        combine(q)

    arrived(g_recv.at[pl.ds(0, nz - 1)], g_rsem.at[groups - 1])
    combine(groups - 1)

    for j in range(2):
        arrived(m_send.at[j, pl.ds(0, owners - 1)], m_ssem.at[j])
        arrived(part.at[j, pl.ds(0, nc - 1)], p_ssem.at[j])
        arrived(whole_recv.at[j, pl.ds(0, nc - 1)], w_ssem.at[j])
    arrived(g_send.at[pl.ds(0, owners - 1)], g_ssem)


def place_kernel(
    assign_hbm, new_ref, update_ref, new_hbm, out_hbm, assign_ref, load_sem, new_sem, out_sem
):
    load = pltpu.make_async_copy(assign_hbm, assign_ref, load_sem)
    load.start()
    copy = pltpu.make_async_copy(update_ref, out_hbm, out_sem)
    copy.start()
    load.wait()

    @pl.loop(0, new_ref.shape[0], unroll=8)
    def _(s):
        pltpu.make_async_copy(new_ref.at[s], new_hbm.at[assign_ref[s]], new_sem).start()

    copy.wait()
    pltpu.make_async_copy(new_ref, new_hbm, new_sem).wait()


def body(momentum, hidden_acts, output_grads, routing, assignment):
    sizes = tuple(lax.axis_size(name) for name in AXES)
    owners = sizes[0] * sizes[1] * sizes[2]
    nc = sizes[3]
    experts, rows, cols = momentum.shape
    tokens, ffe = hidden_acts.shape
    width = cols * nc
    blk = ffe // nc
    scaling = 0.2 * float(max(ffe, width)) ** 0.5
    bf16, f32 = jnp.bfloat16, jnp.float32
    hbm = pl.BlockSpec(memory_space=pltpu.HBM)
    vmem = pl.BlockSpec(memory_space=pltpu.VMEM)
    sem = pltpu.SemaphoreType.DMA
    placed, update = pl.pallas_call(
        functools.partial(exchange_kernel, sizes=sizes, scaling=scaling),
        out_shape=(
            pltpu.VMEM((experts, rows, cols), f32),
            pltpu.VMEM((2, ffe, cols), f32),
        ),
        in_specs=[hbm] * 5,
        out_specs=(vmem, vmem),
        scratch_shapes=[
            pltpu.SMEM((experts,), jnp.int32),
            pltpu.VMEM((1, tokens), jnp.int32),
            pltpu.VMEM((experts, rows, cols), f32),
            pltpu.VMEM((tokens, ffe), bf16),
            pltpu.VMEM((tokens, cols), bf16),
            pltpu.VMEM((2, owners, rows, cols), bf16),
            pltpu.VMEM((2, owners, rows, cols), bf16),
            pltpu.VMEM((owners, 2, rows, cols), bf16),
            pltpu.VMEM((owners, 2, rows, cols), bf16),
            pltpu.VMEM((2, ffe, cols), f32),
            pltpu.VMEM((2, ffe, cols), bf16),
            pltpu.VMEM((2, nc, 5 * blk // 2, blk), bf16),
            pltpu.VMEM((2, nc, 5 * blk // 2, blk), bf16),
            pltpu.VMEM((2, 5 * blk // 2, blk), bf16),
            pltpu.VMEM((2, nc, 5 * blk // 2, blk), bf16),
            pltpu.VMEM((ffe, ffe), bf16),
            pltpu.VMEM((ffe, ffe), bf16),
            pltpu.SemaphoreType.REGULAR((sizes[0] // 2 - 1,)),
            sem((5,)),
            sem((2,)),
            sem((2,)),
            sem(()),
            sem((owners // sizes[0],)),
            sem((2,)),
            sem((2, 2)),
            sem((2,)),
            sem((2, 2)),
        ],
        compiler_params=pltpu.CompilerParams(
            collective_id=0, has_side_effects=True, vmem_limit_bytes=36 << 20
        ),
        name="exchange",
    )(
        pltpu.with_memory_space_constraint(assignment, pltpu.HBM),
        pltpu.with_memory_space_constraint(momentum, pltpu.HBM),
        pltpu.with_memory_space_constraint(hidden_acts, pltpu.HBM),
        pltpu.with_memory_space_constraint(output_grads, pltpu.HBM),
        pltpu.with_memory_space_constraint(routing.reshape(1, tokens), pltpu.HBM),
    )
    return pl.pallas_call(
        place_kernel,
        out_shape=(
            jax.ShapeDtypeStruct((experts, rows, cols), f32),
            jax.ShapeDtypeStruct((2, ffe, cols), f32),
        ),
        in_specs=[hbm, vmem, vmem],
        out_specs=(hbm, hbm),
        scratch_shapes=[pltpu.SMEM((experts,), jnp.int32), sem(()), sem(()), sem(())],
        compiler_params=pltpu.CompilerParams(vmem_limit_bytes=4 << 20),
        name="place",
    )(
        pltpu.with_memory_space_constraint(assignment, pltpu.HBM),
        pltpu.with_memory_space_constraint(placed, pltpu.VMEM),
        pltpu.with_memory_space_constraint(update, pltpu.VMEM),
    )


def solution(mesh):
    owners = mesh.shape["owner"]
    cores = 2 if owners % 2 == 0 else 1
    across = 4 if owners % 8 == 0 else 1
    torus = Mesh(
        mesh.devices.reshape(owners // (across * cores), across, cores, mesh.shape["col"]), AXES
    )
    return jax.shard_map(
        body,
        mesh=torus,
        in_specs=(P(None, OWNER, "col"), P(OWNER, None), P(OWNER, "col"), P(OWNER), P()),
        out_specs=(P(None, OWNER, "col"), P(OWNER, None, "col")),
        check_vma=False,
    )
```

```python
import functools

import jax
import jax.numpy as jnp
from jax import lax
from jax.experimental import pallas as pl
from jax.experimental.pallas import tpu as pltpu
from jax.sharding import Mesh
from jax.sharding import PartitionSpec as P

OWNER = ("owner_0", "owner_1", "owner_2")
AXES = OWNER + ("col",)
MESH = pl.DeviceIdType.MESH

decay_rate = 0.95
epsilon = 1e-07
linear_weight = 3.4445
cubic_weight = -4.775
quintic_weight = 2.0315


def dot(a, b):
    return jnp.dot(a, b, preferred_element_type=jnp.float32)


def dot_rows(a, b):
    return lax.dot_general(a, b, (((1,), (1,)), ((), ())), preferred_element_type=jnp.float32)


def exchange_kernel(
    assign_hbm,
    momentum_hbm,
    hidden_hbm,
    grads_hbm,
    routing_hbm,
    new_ref,
    update_ref,
    assign_ref,
    routing_ref,
    mom,
    hid,
    out_grads,
    m_send,
    m_recv,
    g_send,
    g_recv,
    upd32,
    ub,
    part,
    part_recv,
    whole_send,
    whole_recv,
    gram,
    poly,
    hop_sem,
    load_sem,
    m_ssem,
    m_rsem,
    g_ssem,
    g_rsem,
    p_ssem,
    p_rsem,
    w_ssem,
    w_rsem,
    *,
    sizes,
    scaling,
):
    nz, nx, nk, nc = sizes
    owners = nz * nx * nk
    rows = mom.shape[1]
    ffe = ub.shape[1]
    blk = ffe // nc
    z, x, k, c = (lax.axis_index(name) for name in AXES)
    me = (z * nx + x) * nk + k

    def offsets(n):
        i = n % nz
        w = nx * nk - 1 - n // nz
        dz = nz // 2 + (i % 2) * ((i + 1) // 2) - (1 - i % 2) * (i // 2)
        return dz, w // nk, w % nk

    def sender(n):
        dz, dx, dk = offsets(n)
        return (((z + nz - dz) % nz) * nx + (x + nx - dx) % nx) * nk + (k + nk - dk) % nk

    zs = [lax.rem(z + d, nz) for d in range(nz)]
    xs = [lax.rem(x + d, nx) for d in range(nx)]
    ks = [lax.rem(k + d, nk) for d in range(nk)]
    above, below = (zs[1], x, k, c), (zs[nz - 1], x, k, c)
    barrier = pltpu.get_barrier_semaphore()
    for dx in sorted(range(nx), key=lambda d: -min(d, nx - d)):
        for dk in range(nk - 1, -1, -1):
            for dz in (1, nz - 1, 0):
                if (dz, dx, dk) != (0, 0, 0):
                    pl.semaphore_signal(
                        barrier,
                        inc=1,
                        device_id=(zs[dz], xs[dx], ks[dk], c),
                        device_id_type=MESH,
                    )
    for d in range(1, nc):
        pl.semaphore_signal(
            barrier, inc=1, device_id=(z, x, k, lax.rem(c + d, nc)), device_id_type=MESH
        )

    pairs = (
        (assign_hbm, assign_ref),
        (momentum_hbm, mom),
        (hidden_hbm, hid),
        (grads_hbm, out_grads),
        (routing_hbm, routing_ref),
    )
    loads = [
        pltpu.make_async_copy(source, target, load_sem.at[i])
        for i, (source, target) in enumerate(pairs)
    ]
    for copy in loads:
        copy.start()
    loads[0].wait()
    loads[1].wait()
    def convert(j):
        @pl.loop(0, owners, unroll=4)
        def _(o):
            m_send[j, o] = mom[assign_ref[2 * o + j]].astype(jnp.bfloat16)

    def send_planes(j, planes, first=0):
        @pl.loop(first, nx * nk)
        def _(w):
            px, pk = lax.rem(x + w // nk, nx), lax.rem(k + w % nk, nk)
            for dz in planes:
                pltpu.make_async_remote_copy(
                    src_ref=m_send.at[j, (zs[dz] * nx + px) * nk + pk],
                    dst_ref=m_recv.at[j, me],
                    send_sem=m_ssem.at[j],
                    recv_sem=m_rsem.at[j],
                    device_id=(zs[dz], px, pk, c),
                    device_id_type=MESH,
                ).start()

    convert(0)
    pl.semaphore_wait(barrier, 3 * nx * nk - 1 + nc - 1)
    half = nz // 2
    for d in range(1, half + 1):
        if d > 1:
            pl.semaphore_wait(hop_sem.at[d - 2], 2)
        if d < half:
            for where in (above, below):
                pl.semaphore_signal(
                    hop_sem.at[d - 1], inc=1, device_id=where, device_id_type=MESH
                )
        send_planes(0, [d] if d == half else [d, nz - d])
    send_planes(0, [0], 1)
    convert(1)
    def paced(alpha, send):
        late = [1 - alpha * max(0.0, 1 - p / half) for p in range(nz)]
        turn = [(p % 2) * half + p // 2 for p in range(nz)]
        jobs = [(i, p) for i in range(nx * nk) for p in turn]
        for i, p in sorted(jobs, key=lambda job: (job[0] + 1) * late[job[1]]):
            w = nx * nk - 1 - i
            px, pk = xs[w // nk], ks[w % nk]

            def go(p=p, i=i, px=px, pk=pk):
                send(i, (p * nx + px) * nk + pk, (p, px, pk, c))

            if w > 0:
                go()
            else:
                pl.when(z != p)(go)

    def send_second(i, to, where):
        pltpu.make_async_remote_copy(
            src_ref=m_send.at[1, to],
            dst_ref=m_recv.at[1, me],
            send_sem=m_ssem.at[1],
            recv_sem=m_rsem.at[1],
            device_id=where,
            device_id_type=MESH,
        ).start()

    paced(0.05, send_second)

    for copy in loads[2:]:
        copy.wait()
    hid_t = hid[...].T
    for j in range(2):
        m_recv[j, me] = m_send[j, me]
        chosen = jnp.where(routing_ref[...] == j, hid_t, jnp.zeros((), jnp.bfloat16))
        upd32[j] = dot(chosen, out_grads[...])

        @pl.loop(0, owners, unroll=4)
        def _(o):
            at = pl.multiple_of(o * rows, rows)
            g_send[o, j] = upd32[j, pl.ds(at, rows), :].astype(jnp.bfloat16)

    def send_back(i, to, where):
        pltpu.make_async_remote_copy(
            src_ref=g_send.at[to],
            dst_ref=g_recv.at[me],
            send_sem=g_ssem,
            recv_sem=g_rsem.at[i],
            device_id=where,
            device_id_type=MESH,
        ).start()

    paced(0.15, send_back)

    g_recv[me] = g_send[me]

    depth = part.shape[2] // 2

    def spread(source, target, send, recv, j, h):
        for d in (2, 1, 3):
            to = lax.rem(c + d, nc)
            pltpu.make_async_remote_copy(
                src_ref=source(to),
                dst_ref=target,
                send_sem=send.at[j],
                recv_sem=recv.at[j, h],
                device_id=(z, x, k, to),
                device_id_type=MESH,
            ).start()

    def arrived(ref, sem):
        pltpu.make_async_copy(ref, ref, sem).wait()

    def partial_gram(j):
        arrived(m_recv.at[j, pl.ds(0, owners - 1)], m_rsem.at[j])

        @pl.loop(0, owners, unroll=4)
        def _(o):
            at = pl.multiple_of(o * rows, rows)
            upd32[j, pl.ds(at, rows), :] = decay_rate * m_recv[j, o].astype(
                jnp.float32
            ) + upd32[j, pl.ds(at, rows), :]

        ub[j] = upd32[j].astype(jnp.bfloat16)
        product = dot_rows(ub[j], ub[j])
        product = product.astype(jnp.bfloat16)
        for b in range(nc):
            own = product[b * blk : (b + 1) * blk]
            after = (b + 1) % nc * blk
            top, left = b % 2 * blk + b // 2 * (blk // 2), (b % 2 + 2) * blk
            part[j, b, 0:blk] = own[:, b * blk : (b + 1) * blk]
            part[j, b, blk : 2 * blk] = own[:, after : after + blk]
            part[j, b, 2 * blk :] = product[top : top + blk // 2, left : left + blk]
        for h in range(2):
            piece = pl.ds(h * depth, depth)
            spread(
                lambda to: part.at[j, to, piece], part_recv.at[j, c, piece], p_ssem, p_rsem, j, h
            )
        part_recv[j, c] = part[j, c]

    def sum_parts(j):
        for h in range(2):
            piece = pl.ds(h * depth, depth)
            arrived(part_recv.at[j, pl.ds(0, nc - 1), piece], p_rsem.at[j, h])
            total = part_recv[j, 0, piece].astype(jnp.float32)
            for b in range(1, nc):
                total = total + part_recv[j, b, piece].astype(jnp.float32)
            whole_send[j, piece] = total.astype(jnp.bfloat16)
            spread(
                lambda to: whole_send.at[j, piece],
                whole_recv.at[j, c, piece],
                w_ssem,
                w_rsem,
                j,
                h,
            )
        whole_recv[j, c] = whole_send[j]

    partial_gram(0)
    sum_parts(0)
    partial_gram(1)
    sum_parts(1)

    @pl.loop(0, 2)
    def _(j):
        for h in range(2):
            piece = pl.ds(h * depth, depth)
            arrived(whole_recv.at[j, pl.ds(0, nc - 1), piece], w_rsem.at[j, h])
        eye = lax.broadcasted_iota(jnp.int32, (blk, blk), 0) == lax.broadcasted_iota(
            jnp.int32, (blk, blk), 1
        )
        diagonal = jnp.zeros((blk, blk), jnp.float32)
        for b in range(nc):
            diagonal = diagonal + jnp.where(
                eye, whole_recv[j, b, 0:blk].astype(jnp.float32), 0.0
            )
        squares = jnp.sum(
            jnp.sum(diagonal, axis=0, keepdims=True), axis=1, keepdims=True
        )
        inverse = 1.0 / (jnp.sqrt(squares) + epsilon)

        def scaled(*where):
            return (whole_recv[where].astype(jnp.float32) * inverse) * inverse

        def fill(p, q, block):
            gram[p * blk : (p + 1) * blk, q * blk : (q + 1) * blk] = block.astype(jnp.bfloat16)
            if p != q:
                gram[q * blk : (q + 1) * blk, p * blk : (p + 1) * blk] = block.T.astype(
                    jnp.bfloat16
                )

        for b in range(nc):
            fill(b, b, scaled(j, b, slice(0, blk)))
            fill(b, (b + 1) % nc, scaled(j, b, slice(blk, 2 * blk)))
            if b < 2:
                rest = slice(2 * blk, None)
                fill(b, b + 2, jnp.concatenate([scaled(j, b, rest), scaled(j, b + 2, rest)], 0))
        g1 = gram[...]
        p1 = (cubic_weight * g1.astype(jnp.float32) + quintic_weight * dot(g1, g1)).astype(
            jnp.bfloat16
        )
        poly[...] = p1
        t1 = dot(g1, p1)
        g2 = (
            linear_weight**2 * g1.astype(jnp.float32)
            + 2.0 * linear_weight * t1
            + dot(p1, t1.astype(jnp.bfloat16))
        ).astype(jnp.bfloat16)
        gram[...] = g2
        p2 = (cubic_weight * g2.astype(jnp.float32) + quintic_weight * dot(g2, g2)).astype(
            jnp.bfloat16
        )
        p1 = poly[...]
        rest = (
            linear_weight * (p1.astype(jnp.float32) + p2.astype(jnp.float32)) + dot(p2, p1)
        ).astype(jnp.bfloat16)
        update_ref[j] = (scaling * inverse) * (linear_weight**2 * upd32[j] + dot(rest, ub[j]))

    def combine(q):
        for i in range(nz):
            o = sender(q * nz + i)
            for j in range(2):
                new_ref[2 * o + j] = decay_rate * mom[assign_ref[2 * o + j]] + g_recv[o, j].astype(
                    jnp.float32
                )

    groups = owners // nz

    @pl.loop(0, groups - 1)
    def _(q):
        arrived(g_recv.at[pl.ds(0, nz)], g_rsem.at[q])
        combine(q)

    arrived(g_recv.at[pl.ds(0, nz - 1)], g_rsem.at[groups - 1])
    combine(groups - 1)

    for j in range(2):
        arrived(m_send.at[j, pl.ds(0, owners - 1)], m_ssem.at[j])
        arrived(part.at[j, pl.ds(0, nc - 1)], p_ssem.at[j])
        arrived(whole_recv.at[j, pl.ds(0, nc - 1)], w_ssem.at[j])
    arrived(g_send.at[pl.ds(0, owners - 1)], g_ssem)


def place_kernel(
    assign_hbm, new_ref, update_ref, new_hbm, out_hbm, assign_ref, load_sem, new_sem, out_sem
):
    load = pltpu.make_async_copy(assign_hbm, assign_ref, load_sem)
    load.start()
    copy = pltpu.make_async_copy(update_ref, out_hbm, out_sem)
    copy.start()
    load.wait()

    @pl.loop(0, new_ref.shape[0], unroll=8)
    def _(s):
        pltpu.make_async_copy(new_ref.at[s], new_hbm.at[assign_ref[s]], new_sem).start()

    copy.wait()
    pltpu.make_async_copy(new_ref, new_hbm, new_sem).wait()


def body(momentum, hidden_acts, output_grads, routing, assignment):
    sizes = tuple(lax.axis_size(name) for name in AXES)
    owners = sizes[0] * sizes[1] * sizes[2]
    nc = sizes[3]
    experts, rows, cols = momentum.shape
    tokens, ffe = hidden_acts.shape
    width = cols * nc
    blk = ffe // nc
    scaling = 0.2 * float(max(ffe, width)) ** 0.5
    bf16, f32 = jnp.bfloat16, jnp.float32
    hbm = pl.BlockSpec(memory_space=pltpu.HBM)
    vmem = pl.BlockSpec(memory_space=pltpu.VMEM)
    sem = pltpu.SemaphoreType.DMA
    placed, update = pl.pallas_call(
        functools.partial(exchange_kernel, sizes=sizes, scaling=scaling),
        out_shape=(
            pltpu.VMEM((experts, rows, cols), f32),
            pltpu.VMEM((2, ffe, cols), f32),
        ),
        in_specs=[hbm] * 5,
        out_specs=(vmem, vmem),
        scratch_shapes=[
            pltpu.SMEM((experts,), jnp.int32),
            pltpu.VMEM((1, tokens), jnp.int32),
            pltpu.VMEM((experts, rows, cols), f32),
            pltpu.VMEM((tokens, ffe), bf16),
            pltpu.VMEM((tokens, cols), bf16),
            pltpu.VMEM((2, owners, rows, cols), bf16),
            pltpu.VMEM((2, owners, rows, cols), bf16),
            pltpu.VMEM((owners, 2, rows, cols), bf16),
            pltpu.VMEM((owners, 2, rows, cols), bf16),
            pltpu.VMEM((2, ffe, cols), f32),
            pltpu.VMEM((2, ffe, cols), bf16),
            pltpu.VMEM((2, nc, 5 * blk // 2, blk), bf16),
            pltpu.VMEM((2, nc, 5 * blk // 2, blk), bf16),
            pltpu.VMEM((2, 5 * blk // 2, blk), bf16),
            pltpu.VMEM((2, nc, 5 * blk // 2, blk), bf16),
            pltpu.VMEM((ffe, ffe), bf16),
            pltpu.VMEM((ffe, ffe), bf16),
            pltpu.SemaphoreType.REGULAR((sizes[0] // 2 - 1,)),
            sem((5,)),
            sem((2,)),
            sem((2,)),
            sem(()),
            sem((owners // sizes[0],)),
            sem((2,)),
            sem((2, 2)),
            sem((2,)),
            sem((2, 2)),
        ],
        compiler_params=pltpu.CompilerParams(
            collective_id=0, has_side_effects=True, vmem_limit_bytes=36 << 20
        ),
        name="exchange",
    )(
        pltpu.with_memory_space_constraint(assignment, pltpu.HBM),
        pltpu.with_memory_space_constraint(momentum, pltpu.HBM),
        pltpu.with_memory_space_constraint(hidden_acts, pltpu.HBM),
        pltpu.with_memory_space_constraint(output_grads, pltpu.HBM),
        pltpu.with_memory_space_constraint(routing.reshape(1, tokens), pltpu.HBM),
    )
    return pl.pallas_call(
        place_kernel,
        out_shape=(
            jax.ShapeDtypeStruct((experts, rows, cols), f32),
            jax.ShapeDtypeStruct((2, ffe, cols), f32),
        ),
        in_specs=[hbm, vmem, vmem],
        out_specs=(hbm, hbm),
        scratch_shapes=[pltpu.SMEM((experts,), jnp.int32), sem(()), sem(()), sem(())],
        compiler_params=pltpu.CompilerParams(vmem_limit_bytes=4 << 20),
        name="place",
    )(
        pltpu.with_memory_space_constraint(assignment, pltpu.HBM),
        pltpu.with_memory_space_constraint(placed, pltpu.VMEM),
        pltpu.with_memory_space_constraint(update, pltpu.VMEM),
    )


def solution(mesh):
    owners = mesh.shape["owner"]
    cores = 2 if owners % 2 == 0 else 1
    across = 4 if owners % 8 == 0 else 1
    torus = Mesh(
        mesh.devices.reshape(owners // (across * cores), across, cores, mesh.shape["col"]), AXES
    )
    return jax.shard_map(
        body,
        mesh=torus,
        in_specs=(P(None, OWNER, "col"), P(OWNER, None), P(OWNER, "col"), P(OWNER), P()),
        out_specs=(P(None, OWNER, "col"), P(OWNER, None, "col")),
        check_vma=False,
    )
```

```python
import functools

import jax
import jax.numpy as jnp
from jax import lax
from jax.experimental import pallas as pl
from jax.experimental.pallas import tpu as pltpu
from jax.sharding import Mesh
from jax.sharding import PartitionSpec as P

OWNER = ("owner_0", "owner_1", "owner_2")
AXES = OWNER + ("col",)
MESH = pl.DeviceIdType.MESH

decay_rate = 0.95
epsilon = 1e-07
linear_weight = 3.4445
cubic_weight = -4.775
quintic_weight = 2.0315


def dot(a, b):
    return jnp.dot(a, b, preferred_element_type=jnp.float32)


def dot_rows(a, b):
    return lax.dot_general(a, b, (((1,), (1,)), ((), ())), preferred_element_type=jnp.float32)


def exchange_kernel(
    assign_hbm,
    momentum_hbm,
    hidden_hbm,
    grads_hbm,
    routing_hbm,
    new_ref,
    update_ref,
    assign_ref,
    routing_ref,
    mom,
    hid,
    out_grads,
    m_send,
    m_recv,
    g_send,
    g_recv,
    upd32,
    ub,
    part,
    part_recv,
    whole_send,
    whole_recv,
    gram,
    poly,
    hop_sem,
    load_sem,
    m_ssem,
    m_rsem,
    g_ssem,
    g_rsem,
    p_ssem,
    p_rsem,
    w_ssem,
    w_rsem,
    *,
    sizes,
    scaling,
):
    nz, nx, nk, nc = sizes
    owners = nz * nx * nk
    rows = mom.shape[1]
    ffe = ub.shape[1]
    blk = ffe // nc
    z, x, k, c = (lax.axis_index(name) for name in AXES)
    me = (z * nx + x) * nk + k

    def offsets(n):
        i = n % nz
        w = nx * nk - 1 - n // nz
        dz = nz // 2 + (i % 2) * ((i + 1) // 2) - (1 - i % 2) * (i // 2)
        return dz, w // nk, w % nk

    def sender(n):
        dz, dx, dk = offsets(n)
        return (((z + nz - dz) % nz) * nx + (x + nx - dx) % nx) * nk + (k + nk - dk) % nk

    pairs = (
        (assign_hbm, assign_ref),
        (momentum_hbm, mom),
        (hidden_hbm, hid),
        (grads_hbm, out_grads),
        (routing_hbm, routing_ref),
    )
    loads = [
        pltpu.make_async_copy(source, target, load_sem.at[i])
        for i, (source, target) in enumerate(pairs)
    ]
    for copy in loads[:2]:
        copy.start()
    zs = [lax.rem(z + d, nz) for d in range(nz)]
    xs = [lax.rem(x + d, nx) for d in range(nx)]
    ks = [lax.rem(k + d, nk) for d in range(nk)]
    above, below = (zs[1], x, k, c), (zs[nz - 1], x, k, c)
    barrier = pltpu.get_barrier_semaphore()
    for dx in sorted(range(nx), key=lambda d: -min(d, nx - d)):
        for dk in range(nk - 1, -1, -1):
            for dz in (1, nz - 1, 0):
                if (dz, dx, dk) != (0, 0, 0):
                    pl.semaphore_signal(
                        barrier,
                        inc=1,
                        device_id=(zs[dz], xs[dx], ks[dk], c),
                        device_id_type=MESH,
                    )
    for d in range(1, nc):
        pl.semaphore_signal(
            barrier, inc=1, device_id=(z, x, k, lax.rem(c + d, nc)), device_id_type=MESH
        )

    loads[0].wait()
    loads[1].wait()
    def convert(j):
        @pl.loop(0, owners, unroll=4)
        def _(o):
            m_send[j, o] = mom[assign_ref[2 * o + j]].astype(jnp.bfloat16)

    def send_planes(j, planes, first=0):
        @pl.loop(first, nx * nk)
        def _(w):
            px, pk = lax.rem(x + w // nk, nx), lax.rem(k + w % nk, nk)
            for dz in planes:
                pltpu.make_async_remote_copy(
                    src_ref=m_send.at[j, (zs[dz] * nx + px) * nk + pk],
                    dst_ref=m_recv.at[j, me],
                    send_sem=m_ssem.at[j],
                    recv_sem=m_rsem.at[j],
                    device_id=(zs[dz], px, pk, c),
                    device_id_type=MESH,
                ).start()

    convert(0)
    for copy in loads[2:]:
        copy.start()
    pl.semaphore_wait(barrier, 3 * nx * nk - 1 + nc - 1)
    half = nz // 2
    for d in range(1, half + 1):
        if d > 1:
            pl.semaphore_wait(hop_sem.at[d - 2], 2)
        if d < half:
            for where in (above, below):
                pl.semaphore_signal(
                    hop_sem.at[d - 1], inc=1, device_id=where, device_id_type=MESH
                )
        send_planes(0, [d] if d == half else [d, nz - d])
    send_planes(0, [0], 1)
    convert(1)
    def paced(alpha, send):
        late = [1 - alpha * max(0.0, 1 - p / half) for p in range(nz)]
        turn = [(p % 2) * half + p // 2 for p in range(nz)]
        jobs = [(i, p) for i in range(nx * nk) for p in turn]
        for i, p in sorted(jobs, key=lambda job: (job[0] + 1) * late[job[1]]):
            w = nx * nk - 1 - i
            px, pk = xs[w // nk], ks[w % nk]

            def go(p=p, i=i, px=px, pk=pk):
                send(i, (p * nx + px) * nk + pk, (p, px, pk, c))

            if w > 0:
                go()
            else:
                pl.when(z != p)(go)

    def send_second(i, to, where):
        pltpu.make_async_remote_copy(
            src_ref=m_send.at[1, to],
            dst_ref=m_recv.at[1, me],
            send_sem=m_ssem.at[1],
            recv_sem=m_rsem.at[1],
            device_id=where,
            device_id_type=MESH,
        ).start()

    paced(0.05, send_second)

    for copy in loads[2:]:
        copy.wait()
    hid_t = hid[...].T
    for j in range(2):
        m_recv[j, me] = m_send[j, me]
        chosen = jnp.where(routing_ref[...] == j, hid_t, jnp.zeros((), jnp.bfloat16))
        upd32[j] = dot(chosen, out_grads[...])

        @pl.loop(0, owners, unroll=4)
        def _(o):
            at = pl.multiple_of(o * rows, rows)
            g_send[o, j] = upd32[j, pl.ds(at, rows), :].astype(jnp.bfloat16)

    def send_back(i, to, where):
        pltpu.make_async_remote_copy(
            src_ref=g_send.at[to],
            dst_ref=g_recv.at[me],
            send_sem=g_ssem,
            recv_sem=g_rsem.at[i],
            device_id=where,
            device_id_type=MESH,
        ).start()

    paced(0.15, send_back)

    g_recv[me] = g_send[me]

    depth = part.shape[2] // 2

    def spread(source, target, send, recv, j, h):
        for d in (2, 1, 3):
            to = lax.rem(c + d, nc)
            pltpu.make_async_remote_copy(
                src_ref=source(to),
                dst_ref=target,
                send_sem=send.at[j],
                recv_sem=recv.at[j, h],
                device_id=(z, x, k, to),
                device_id_type=MESH,
            ).start()

    def arrived(ref, sem):
        pltpu.make_async_copy(ref, ref, sem).wait()

    def partial_gram(j):
        arrived(m_recv.at[j, pl.ds(0, owners - 1)], m_rsem.at[j])

        @pl.loop(0, owners, unroll=4)
        def _(o):
            at = pl.multiple_of(o * rows, rows)
            upd32[j, pl.ds(at, rows), :] = decay_rate * m_recv[j, o].astype(
                jnp.float32
            ) + upd32[j, pl.ds(at, rows), :]

        ub[j] = upd32[j].astype(jnp.bfloat16)
        product = dot_rows(ub[j], ub[j])
        product = product.astype(jnp.bfloat16)
        for b in range(nc):
            own = product[b * blk : (b + 1) * blk]
            after = (b + 1) % nc * blk
            top, left = b % 2 * blk + b // 2 * (blk // 2), (b % 2 + 2) * blk
            part[j, b, 0:blk] = own[:, b * blk : (b + 1) * blk]
            part[j, b, blk : 2 * blk] = own[:, after : after + blk]
            part[j, b, 2 * blk :] = product[top : top + blk // 2, left : left + blk]
        for h in range(2):
            piece = pl.ds(h * depth, depth)
            spread(
                lambda to: part.at[j, to, piece], part_recv.at[j, c, piece], p_ssem, p_rsem, j, h
            )
        part_recv[j, c] = part[j, c]

    def sum_parts(j):
        for h in range(2):
            piece = pl.ds(h * depth, depth)
            arrived(part_recv.at[j, pl.ds(0, nc - 1), piece], p_rsem.at[j, h])
            total = part_recv[j, 0, piece].astype(jnp.float32)
            for b in range(1, nc):
                total = total + part_recv[j, b, piece].astype(jnp.float32)
            whole_send[j, piece] = total.astype(jnp.bfloat16)
            spread(
                lambda to: whole_send.at[j, piece],
                whole_recv.at[j, c, piece],
                w_ssem,
                w_rsem,
                j,
                h,
            )
        whole_recv[j, c] = whole_send[j]

    partial_gram(0)
    sum_parts(0)
    partial_gram(1)
    sum_parts(1)

    @pl.loop(0, 2)
    def _(j):
        for h in range(2):
            piece = pl.ds(h * depth, depth)
            arrived(whole_recv.at[j, pl.ds(0, nc - 1), piece], w_rsem.at[j, h])
        eye = lax.broadcasted_iota(jnp.int32, (blk, blk), 0) == lax.broadcasted_iota(
            jnp.int32, (blk, blk), 1
        )
        diagonal = jnp.zeros((blk, blk), jnp.float32)
        for b in range(nc):
            diagonal = diagonal + jnp.where(
                eye, whole_recv[j, b, 0:blk].astype(jnp.float32), 0.0
            )
        squares = jnp.sum(
            jnp.sum(diagonal, axis=0, keepdims=True), axis=1, keepdims=True
        )
        inverse = 1.0 / (jnp.sqrt(squares) + epsilon)

        def scaled(*where):
            return (whole_recv[where].astype(jnp.float32) * inverse) * inverse

        def fill(p, q, block):
            gram[p * blk : (p + 1) * blk, q * blk : (q + 1) * blk] = block.astype(jnp.bfloat16)
            if p != q:
                gram[q * blk : (q + 1) * blk, p * blk : (p + 1) * blk] = block.T.astype(
                    jnp.bfloat16
                )

        for b in range(nc):
            fill(b, b, scaled(j, b, slice(0, blk)))
            fill(b, (b + 1) % nc, scaled(j, b, slice(blk, 2 * blk)))
            if b < 2:
                rest = slice(2 * blk, None)
                fill(b, b + 2, jnp.concatenate([scaled(j, b, rest), scaled(j, b + 2, rest)], 0))
        g1 = gram[...]
        p1 = (cubic_weight * g1.astype(jnp.float32) + quintic_weight * dot(g1, g1)).astype(
            jnp.bfloat16
        )
        poly[...] = p1
        t1 = dot(g1, p1)
        g2 = (
            linear_weight**2 * g1.astype(jnp.float32)
            + 2.0 * linear_weight * t1
            + dot(p1, t1.astype(jnp.bfloat16))
        ).astype(jnp.bfloat16)
        gram[...] = g2
        p2 = (cubic_weight * g2.astype(jnp.float32) + quintic_weight * dot(g2, g2)).astype(
            jnp.bfloat16
        )
        p1 = poly[...]
        rest = (
            linear_weight * (p1.astype(jnp.float32) + p2.astype(jnp.float32)) + dot(p2, p1)
        ).astype(jnp.bfloat16)
        update_ref[j] = (scaling * inverse) * (linear_weight**2 * upd32[j] + dot(rest, ub[j]))

    def combine(q):
        for i in range(nz):
            o = sender(q * nz + i)
            for j in range(2):
                new_ref[2 * o + j] = decay_rate * mom[assign_ref[2 * o + j]] + g_recv[o, j].astype(
                    jnp.float32
                )

    groups = owners // nz

    @pl.loop(0, groups - 1)
    def _(q):
        arrived(g_recv.at[pl.ds(0, nz)], g_rsem.at[q])
        combine(q)

    arrived(g_recv.at[pl.ds(0, nz - 1)], g_rsem.at[groups - 1])
    combine(groups - 1)

    for j in range(2):
        arrived(m_send.at[j, pl.ds(0, owners - 1)], m_ssem.at[j])
        arrived(part.at[j, pl.ds(0, nc - 1)], p_ssem.at[j])
        arrived(whole_recv.at[j, pl.ds(0, nc - 1)], w_ssem.at[j])
    arrived(g_send.at[pl.ds(0, owners - 1)], g_ssem)


def place_kernel(
    assign_hbm, new_ref, update_ref, new_hbm, out_hbm, assign_ref, load_sem, new_sem, out_sem
):
    load = pltpu.make_async_copy(assign_hbm, assign_ref, load_sem)
    load.start()
    copy = pltpu.make_async_copy(update_ref, out_hbm, out_sem)
    copy.start()
    load.wait()

    @pl.loop(0, new_ref.shape[0], unroll=8)
    def _(s):
        pltpu.make_async_copy(new_ref.at[s], new_hbm.at[assign_ref[s]], new_sem).start()

    copy.wait()
    pltpu.make_async_copy(new_ref, new_hbm, new_sem).wait()


def body(momentum, hidden_acts, output_grads, routing, assignment):
    sizes = tuple(lax.axis_size(name) for name in AXES)
    owners = sizes[0] * sizes[1] * sizes[2]
    nc = sizes[3]
    experts, rows, cols = momentum.shape
    tokens, ffe = hidden_acts.shape
    width = cols * nc
    blk = ffe // nc
    scaling = 0.2 * float(max(ffe, width)) ** 0.5
    bf16, f32 = jnp.bfloat16, jnp.float32
    hbm = pl.BlockSpec(memory_space=pltpu.HBM)
    vmem = pl.BlockSpec(memory_space=pltpu.VMEM)
    sem = pltpu.SemaphoreType.DMA
    placed, update = pl.pallas_call(
        functools.partial(exchange_kernel, sizes=sizes, scaling=scaling),
        out_shape=(
            pltpu.VMEM((experts, rows, cols), f32),
            pltpu.VMEM((2, ffe, cols), f32),
        ),
        in_specs=[hbm] * 5,
        out_specs=(vmem, vmem),
        scratch_shapes=[
            pltpu.SMEM((experts,), jnp.int32),
            pltpu.VMEM((1, tokens), jnp.int32),
            pltpu.VMEM((experts, rows, cols), f32),
            pltpu.VMEM((tokens, ffe), bf16),
            pltpu.VMEM((tokens, cols), bf16),
            pltpu.VMEM((2, owners, rows, cols), bf16),
            pltpu.VMEM((2, owners, rows, cols), bf16),
            pltpu.VMEM((owners, 2, rows, cols), bf16),
            pltpu.VMEM((owners, 2, rows, cols), bf16),
            pltpu.VMEM((2, ffe, cols), f32),
            pltpu.VMEM((2, ffe, cols), bf16),
            pltpu.VMEM((2, nc, 5 * blk // 2, blk), bf16),
            pltpu.VMEM((2, nc, 5 * blk // 2, blk), bf16),
            pltpu.VMEM((2, 5 * blk // 2, blk), bf16),
            pltpu.VMEM((2, nc, 5 * blk // 2, blk), bf16),
            pltpu.VMEM((ffe, ffe), bf16),
            pltpu.VMEM((ffe, ffe), bf16),
            pltpu.SemaphoreType.REGULAR((sizes[0] // 2 - 1,)),
            sem((5,)),
            sem((2,)),
            sem((2,)),
            sem(()),
            sem((owners // sizes[0],)),
            sem((2,)),
            sem((2, 2)),
            sem((2,)),
            sem((2, 2)),
        ],
        compiler_params=pltpu.CompilerParams(
            collective_id=0, has_side_effects=True, vmem_limit_bytes=36 << 20
        ),
        name="exchange",
    )(
        pltpu.with_memory_space_constraint(assignment, pltpu.HBM),
        pltpu.with_memory_space_constraint(momentum, pltpu.HBM),
        pltpu.with_memory_space_constraint(hidden_acts, pltpu.HBM),
        pltpu.with_memory_space_constraint(output_grads, pltpu.HBM),
        pltpu.with_memory_space_constraint(routing.reshape(1, tokens), pltpu.HBM),
    )
    return pl.pallas_call(
        place_kernel,
        out_shape=(
            jax.ShapeDtypeStruct((experts, rows, cols), f32),
            jax.ShapeDtypeStruct((2, ffe, cols), f32),
        ),
        in_specs=[hbm, vmem, vmem],
        out_specs=(hbm, hbm),
        scratch_shapes=[pltpu.SMEM((experts,), jnp.int32), sem(()), sem(()), sem(())],
        compiler_params=pltpu.CompilerParams(vmem_limit_bytes=4 << 20),
        name="place",
    )(
        pltpu.with_memory_space_constraint(assignment, pltpu.HBM),
        pltpu.with_memory_space_constraint(placed, pltpu.VMEM),
        pltpu.with_memory_space_constraint(update, pltpu.VMEM),
    )


def solution(mesh):
    owners = mesh.shape["owner"]
    cores = 2 if owners % 2 == 0 else 1
    across = 4 if owners % 8 == 0 else 1
    torus = Mesh(
        mesh.devices.reshape(owners // (across * cores), across, cores, mesh.shape["col"]), AXES
    )
    return jax.shard_map(
        body,
        mesh=torus,
        in_specs=(P(None, OWNER, "col"), P(OWNER, None), P(OWNER, "col"), P(OWNER), P()),
        out_specs=(P(None, OWNER, "col"), P(OWNER, None, "col")),
        check_vma=False,
    )
```
